128 devices in a mesh: gx: 16 (over z, y_lo, core), gy: 8 (over y_hi, x).
Axes of the slice: x: 4, y: 4 (y_hi: 2, y_lo: 2; y = y_hi * 2 + y_lo), z: 4, core: 2. Of those that a mesh axis runs over, the one named last changes fastest.
Arguments:
- water_state: float32 [3, 2048, 4096], P(None, 'gy', 'gx'), may hold values from -0.1 to 1, as said below
- ground: float32 [2048, 4096], P('gy', 'gx'), may hold values from 0 to 0.3
- log_rough: float32 [2048, 4096], P('gy', 'gx'), may hold values from -3.5 to -1.6
- moment: float32 [2048, 4096], P('gy', 'gx'), may hold values from -3 to 3
- second: float32 [2048, 4096], P('gy', 'gx'), may hold values from 0.001 to 1
- wet_tiles: int32 [16, 32], P('gy', 'gx'), may hold values from 0 to 1, as said below
- cotangent: float32 [3, 2048, 4096], P(None, 'gy', 'gx'), may hold values from -2400 to 2400
Outputs:
- new_rough: float32 [2048, 4096], P('gy', 'gx')
- new_moment: float32 [2048, 4096], P('gy', 'gx')
- new_second: float32 [2048, 4096], P('gy', 'gx')
The draws below stay inside these ranges and needn't reach their ends.
Inputs may be any that keep to these rules, and one draw needn't show every extreme that they name: `water_state`: depths (first field) lie in 0.2 to 1.0, discharges in -0.1 to 0.1. `wet_tiles`: two devices of one gy index whose gx indices differ by half of the gx axis form a pair; a pair holds at most 6 wet tiles together, and in every draw some pair holds exactly 6, one of its devices with all its tiles wet.
All inputs are finite; a program needn't handle non-finite values.
Results may differ from the reference program's by a relative error of at most 0.0003.
Values sent between devices are 32-bit elements; how exact they have to be, the bound alone decides.
No kernel may reach another device: no remote copies, remote signals or barrier semaphores. Data moves between devices by JAX's collectives and lax.ppermute only.
A program may use at most 64 MiB of HBM per device.

```python
import math
import jax
import jax.numpy as jnp

TILE = 128
TR_DEV = 2
TC_DEV = 2
LOAD = 3
STEPS = 2
UPDATES = 20
ROWS = 2048
COLS = 4096
N_GX = 16
N_GY = 8


def draw_water_state(key, part):
    depth_key, flow_key = jax.random.split(key)
    depth_now = jax.random.uniform(depth_key, (ROWS, COLS), jnp.float32, minval=0.2, maxval=1.0)
    flows = jax.random.uniform(flow_key, (2, ROWS, COLS), jnp.float32, minval=-0.1, maxval=0.1)
    return jnp.concatenate([depth_now[None], flows], 0)


def draw_wet_tiles(key, part):
    tile_count = TR_DEV * TC_DEV
    half_axis = N_GX // 2
    heavy_key, light_key, side_key, score_key = jax.random.split(jax.random.fold_in(key, 7), 4)
    heavy = jax.random.randint(heavy_key, (N_GY, half_axis), LOAD, tile_count + 1)
    heavy = heavy.at[0, 0].set(tile_count)
    light = jax.random.randint(light_key, (N_GY, half_axis), 0, 2 * LOAD - heavy + 1)
    light = light.at[0, 0].set(2 * LOAD - tile_count)
    side = jax.random.randint(side_key, (N_GY, half_axis), 0, 2)
    lower = jnp.where(side > 0, heavy, light)
    upper = jnp.where(side > 0, light, heavy)
    counts = jnp.concatenate([lower, upper], 1)
    scores = jax.random.randint(score_key, (N_GY, N_GX, tile_count), 0, 1 << 20) * tile_count + jnp.arange(tile_count, dtype=jnp.int32)
    ranks = jnp.argsort(jnp.argsort(scores, axis=-1, stable=True), axis=-1, stable=True)
    wet = (ranks < counts[:, :, None]).astype(jnp.int32)
    wet = wet.reshape(N_GY, N_GX, TR_DEV, TC_DEV).transpose(0, 2, 1, 3)
    return wet.reshape(N_GY * TR_DEV, N_GX * TC_DEV)


def shard_levels(own_key, dims, cuts, smallest, high):
    def one(axis_at, parts):
        draws = jax.random.uniform(jax.random.fold_in(jax.random.fold_in(own_key, 6), axis_at), (parts,), jnp.float32, smallest / len(cuts), high / len(cuts))
        return jnp.repeat(jnp.exp(draws), dims[axis_at] // parts).reshape((-1,) + (1,) * (len(dims) - axis_at - 1))

    loudness = one(*cuts[0])
    for cut in cuts[1:]:
        loudness = loudness * one(*cut)
    return loudness


def scatter_about(stream_key, dims, deviation, most, shards=(), held_as=jnp.bfloat16):
    gain = shard_levels(stream_key, dims, shards, -0.22, 0.18) if shards else 1.0
    array = jax.random.normal(stream_key, dims, jnp.float32) * deviation * gain
    return jnp.minimum(jnp.maximum(array, -most), most).astype(held_as)


def setup_inputs(seed: int = 0) -> dict:
    arg_keys = jax.random.split(jax.random.key(seed), 8)
    return {
        "water_state": draw_water_state(jax.random.fold_in(arg_keys[7], 71), 0),
        "ground": jnp.clip(0.3 * jax.random.uniform(arg_keys[1], (ROWS, COLS), jnp.float32) ** shard_levels(arg_keys[1], (ROWS, COLS), ((0, 8), (1, 16)), -0.2, 0.2), 0.0, 0.3),
        "log_rough": jnp.clip(-3.5 + 1.9 * jax.random.uniform(arg_keys[2], (ROWS, COLS), jnp.float32) ** shard_levels(arg_keys[2], (ROWS, COLS), ((0, 8), (1, 16)), -0.2, 0.2), -3.5, -1.6),
        "moment": scatter_about(arg_keys[3], (ROWS, COLS), 0.5, 3.0, ((0, 8), (1, 16)), jnp.float32),
        "second": jnp.clip(jnp.exp(math.log(1.0) - 6.9077552 * jax.random.uniform(arg_keys[4], (ROWS, COLS), jnp.float32) ** shard_levels(arg_keys[4], (ROWS, COLS), ((0, 8), (1, 16)), -0.2, 0.2)), 0.001, 1.0),
        "wet_tiles": draw_wet_tiles(jax.random.fold_in(arg_keys[7], 71), 0),
        "cotangent": scatter_about(arg_keys[6], (3, ROWS, COLS), 400.0, 2400.0, ((1, 8), (2, 16)), jnp.float32),
    }


GRAVITY = 9.81
COURANT = 0.1
GRAVITY_DT = 9.81
SPEED_EPS = 0.0001
BETA_ONE = 0.9
BETA_TWO = 0.999
LEARN_RATE = 0.05
ATAN_SCALE = 1.27

def mirror_pad(water, ground):
    fields = jnp.concatenate([water, ground[None]], 0)
    padded = jnp.pad(fields, ((0, 0), (1, 1), (1, 1)), mode='edge')
    padded = padded.at[1, :, 0].multiply(-1.0).at[1, :, -1].multiply(-1.0)
    padded = padded.at[2, 0, :].multiply(-1.0).at[2, -1, :].multiply(-1.0)
    return padded

def mean_four(field):
    return 0.25 * (field[1:-1, 2:] + field[1:-1, :-2] + field[2:, 1:-1] + field[:-2, 1:-1])

def diff_cols(field):
    return field[:, 2:] - field[:, :-2]

def diff_rows(field):
    return field[2:, :] - field[:-2, :]

def flux_step(padded):
    depth_now, east_flow, south_flow, ground = (padded[0], padded[1], padded[2], padded[3])
    half_step = 0.5 * COURANT
    row_depth, row_east, row_south = (depth_now[1:-1, :], east_flow[1:-1, :], south_flow[1:-1, :])
    col_depth, col_east, col_south = (depth_now[:, 1:-1], east_flow[:, 1:-1], south_flow[:, 1:-1])
    inner_depth = depth_now[1:-1, 1:-1]
    new_depth = mean_four(depth_now) - half_step * (diff_cols(row_east) + diff_rows(col_south))
    new_east = mean_four(east_flow) - half_step * (diff_cols(row_east * row_east / row_depth + 0.5 * GRAVITY * row_depth * row_depth) + diff_rows(col_east * col_south / col_depth)) - half_step * GRAVITY * inner_depth * diff_cols(ground[1:-1, :])
    new_south = mean_four(south_flow) - half_step * (diff_cols(row_east * row_south / row_depth) + diff_rows(col_south * col_south / col_depth + 0.5 * GRAVITY * col_depth * col_depth)) - half_step * GRAVITY * inner_depth * diff_rows(ground[:, 1:-1])
    return jnp.stack([new_depth, new_east, new_south])

def friction(pre_state, log_rough):
    depth_now, east_flow, south_flow = (pre_state[0], pre_state[1], pre_state[2])
    speed = jnp.sqrt(east_flow * east_flow + south_flow * south_flow + SPEED_EPS)
    drag = 1.0 + GRAVITY_DT * jnp.exp(2.0 * log_rough) * speed * jnp.power(depth_now, -7.0 / 3.0)
    return jnp.stack([depth_now, east_flow / drag, south_flow / drag])

def forward(log_rough, water, ground, wet_cells):
    for step_index in range(STEPS):
        stepped = friction(flux_step(mirror_pad(water, ground)), log_rough)
        water = jnp.where(wet_cells[None], stepped, water)
    return water

def reference(water_state, ground, log_rough, moment, second, wet_tiles, cotangent):
    wet_cells = jnp.repeat(jnp.repeat(wet_tiles, TILE, 0), TILE, 1) > 0
    _, pullback = jax.vjp(lambda rough: forward(rough, water_state, ground, wet_cells), log_rough)
    gradient = pullback(cotangent)[0]
    new_moment = BETA_ONE * moment + (1.0 - BETA_ONE) * gradient
    new_second = BETA_TWO * second + (1.0 - BETA_TWO) * gradient * gradient
    direction = jnp.arctan2(new_moment / (1.0 - BETA_ONE ** UPDATES), jnp.sqrt(new_second / (1.0 - BETA_TWO ** UPDATES)))
    new_rough = log_rough - LEARN_RATE * ATAN_SCALE * direction
    return (new_rough, new_moment, new_second)
```

```python
import functools
import math

import jax
import jax.numpy as jnp
from jax import lax
from jax.experimental import pallas as pl
from jax.experimental.pallas import tpu as pltpu
from jax.sharding import PartitionSpec as P

UPDATES = 20
GRAVITY = 9.81
HALF_STEP = 0.05
LOG_DRAG = math.log(9.81)
SPEED_EPS = 0.0001
BETA_ONE = 0.9
BETA_TWO = 0.999
LEARN_RATE = 0.05
ATAN_SCALE = 1.27
H, QX, QY, Z, LR, CH, CX, CY, WET = range(9)
NF = 9
TURNED = (H, QY, QX, Z, LR, CH, CY, CX, WET)
BLK = 8
VMEM_MB = 12


def from_prev_row(prev, cur):
    row = lax.broadcasted_iota(jnp.int32, cur.shape, 0)
    return pltpu.roll(jnp.where(row == cur.shape[0] - 1, prev, cur), 1, 0)


def from_next_row(cur, nxt):
    row = lax.broadcasted_iota(jnp.int32, cur.shape, 0)
    return pltpu.roll(jnp.where(row == 0, nxt, cur), cur.shape[0] - 1, 0)


def from_prev_col(x):
    return pltpu.roll(x, 1, 1)


def from_next_col(x):
    return pltpu.roll(x, x.shape[1] - 1, 1)


def flux_parts(h, qx, qy, slope_x, slope_y):
    inv = 1.0 / h
    u, v = qx * inv, qy * inv
    press = (0.5 * GRAVITY) * h * h
    k = HALF_STEP
    fx1, fy1 = k * qx, k * qy
    fx2, fxy, fy3 = k * (qx * u + press), k * (qx * v), k * (qy * v + press)
    h4, x4, y4 = 0.25 * h, 0.25 * qx, 0.25 * qy
    cols = [
        from_prev_col(h4 + fx1) + from_next_col(h4 - fx1),
        from_prev_col(x4 + fx2) + from_next_col(x4 - fx2) - h * slope_x,
        from_prev_col(y4 + fxy) + from_next_col(y4 - fxy) - h * slope_y,
    ]
    down = [h4 + fy1, x4 + fxy, y4 + fy3]
    up = [h4 - fy1, x4 - fxy, y4 - fy3]
    return cols, down, up, u, v


def drag_parts(h, qx, qy, rough):
    s2 = qx * qx + qy * qy + SPEED_EPS
    rs = lax.rsqrt(s2)
    b = jnp.exp(2.0 * rough + LOG_DRAG - (7.0 / 3.0) * jnp.log(h)) * (s2 * rs)
    w = 1.0 / (1.0 + b)
    return b, w, rs * rs


def gradient_passes(get, wet, n, lanes, scr, put_grad):
    SX, SY, UH, UX, UY, GA, GB, PH, PX, PY = range(10)

    def rows(i):
        return pl.ds(pl.multiple_of(i * BLK, BLK), BLK)

    def slopes(i):
        z = get(Z, i)
        zp, zn = get(Z, jnp.maximum(i - 1, 0)), get(Z, jnp.minimum(i + 1, n - 1))
        kg = HALF_STEP * GRAVITY
        sx = kg * (from_next_col(z) - from_prev_col(z))
        sy = kg * (from_next_row(z, zn) - from_prev_row(zp, z))
        return sx, sy

    def first_parts(i):
        sx, sy = slopes(i)
        scr[SX, rows(i), :] = sx
        scr[SY, rows(i), :] = sy
        cols, down, up, _, _ = flux_parts(get(H, i), get(QX, i), get(QY, i), sx, sy)
        return cols, down, up

    def first(i, carry):
        dprev, dcur, ucur, ccur = carry
        cols, down, up = first_parts(jnp.minimum(i + 1, n - 1))
        h, qx, qy = [
            from_prev_row(dprev[f], dcur[f]) + from_next_row(ucur[f], up[f]) + ccur[f]
            for f in range(3)
        ]
        b, w, _ = drag_parts(h, qx, qy, get(LR, i))
        m = wet(i)
        scr[UH, rows(i), :] = jnp.where(m, h, get(H, i))
        scr[UX, rows(i), :] = jnp.where(m, qx * w, get(QX, i))
        scr[UY, rows(i), :] = jnp.where(m, qy * w, get(QY, i))
        t = jnp.where(m, -2.0 * b * w * w, 0.0)
        scr[GA, rows(i), :] = t * qx
        scr[GB, rows(i), :] = t * qy
        return dcur, down, up, cols

    cols, down, up = first_parts(0)
    lax.fori_loop(0, n, first, (down, down, up, cols))

    def second_parts(i):
        r = rows(i)
        cols, down, up, u, v = flux_parts(
            scr[UH, r, :], scr[UX, r, :], scr[UY, r, :], scr[SX, r, :], scr[SY, r, :]
        )
        return cols, down, up, u, v

    def second(i, carry):
        dprev, dcur, ucur, ccur, u, v = carry
        cols, down, up, un, vn = second_parts(jnp.minimum(i + 1, n - 1))
        h, qx, qy = [
            from_prev_row(dprev[f], dcur[f]) + from_next_row(ucur[f], up[f]) + ccur[f]
            for f in range(3)
        ]
        b, w, inv_s2 = drag_parts(h, qx, qy, get(LR, i))
        m = wet(i)
        ch, cx, cy = get(CH, i), get(CX, i), get(CY, i)
        t = (cx * qx + cy * qy) * (w * w) * b
        ts = t * inv_s2
        scr[PH, rows(i), :] = jnp.where(m, ch + (7.0 / 3.0) * t / h, 0.0)
        scr[PX, rows(i), :] = jnp.where(m, cx * w - ts * qx, 0.0)
        scr[PY, rows(i), :] = jnp.where(m, cy * w - ts * qy, 0.0)
        put_grad(rows(i), jnp.where(m, -2.0 * t, 0.0), None)
        scr[SX, rows(i), :] = u
        scr[SY, rows(i), :] = v
        return dcur, down, up, cols, un, vn

    cols, down, up, u, v = second_parts(0)
    lax.fori_loop(0, n, second, (down, down, up, cols, u, v))

    def third(i, carry):
        r = rows(i)
        rp, rn = rows(jnp.maximum(i - 1, 0)), rows(jnp.minimum(i + 1, n - 1))
        ph, px, py = scr[PH, r, :], scr[PX, r, :], scr[PY, r, :]

        def four(f, cur):
            return (
                from_next_col(cur),
                from_prev_col(cur),
                from_next_row(cur, scr[f, rn, :]),
                from_prev_row(scr[f, rp, :], cur),
            )

        he, hw, hs, hn = four(PH, ph)
        xe, xw, xs, xn = four(PX, px)
        ye, yw, ys, yn = four(PY, py)
        u, v = scr[SX, r, :], scr[SY, r, :]
        k = HALF_STEP
        cross = k * ((ye - yw) + (xs - xn))
        cot_x = (
            0.25 * ((xe + xw) + (xs + xn))
            + k * (he - hw)
            + (2.0 * k) * u * (xe - xw)
            + v * cross
        )
        cot_y = (
            0.25 * ((ye + yw) + (ys + yn))
            + k * (hs - hn)
            + (2.0 * k) * v * (ys - yn)
            + u * cross
        )
        put_grad(r, None, scr[GA, r, :] * cot_x + scr[GB, r, :] * cot_y)
        return carry

    lax.fori_loop(0, n, third, 0)


def wet_rows(wet_ref, tile_row, shape, tile):
    lane = lax.broadcasted_iota(jnp.int32, shape, 1)
    left = (wet_ref[tile_row, 0] > 0).astype(jnp.float32)
    right = (wet_ref[tile_row, 1] > 0).astype(jnp.float32)
    return jnp.where(lane < tile, left, right)


def place(axis):
    index = lax.axis_index(axis)
    return index, lax.axis_size(axis)


def three_rows(block, first, mirrored, sign):
    natural = block[first : first + 3, :]
    reverse = jnp.concatenate([block[first + 2 - d : first + 3 - d, :] for d in range(3)], 0)
    return jnp.where(mirrored, sign * reverse, natural)


def pack_rows_kernel(wet_ref, wt, wb, gt, gb, lt, lb, ct, cb, a_ref, b_ref):
    gy, ny = place("gy")
    even = gy % 2 == 0
    a_ref[...] = jnp.zeros_like(a_ref)
    b_ref[...] = jnp.zeros_like(b_ref)
    tile = a_ref.shape[1] // 2
    shape = (8, a_ref.shape[1])
    top = [wt[0], wt[1], wt[2], gt[...], lt[...], ct[0], ct[1], ct[2], wet_rows(wet_ref, 0, shape, tile)]
    bot = [wb[0], wb[1], wb[2], gb[...], lb[...], cb[0], cb[1], cb[2], wet_rows(wet_ref, 1, shape, tile)]
    for f in range(NF):
        sign = -1.0 if f in (QY, CY) else 1.0
        t = three_rows(top[f], 0, gy == 0, sign)
        b = three_rows(bot[f], 5, gy == ny - 1, sign)
        a_ref[3 * f : 3 * f + 3, :] = jnp.where(even, b, t)
        b_ref[3 * f : 3 * f + 3, :] = jnp.where(even, t, b)


def inner_kernel(wet_ref, w_ref, z_ref, lr_ref, c_ref, g_ref, rs_ref, tl_ref, tr_ref, scr):
    height, lanes = z_ref.shape
    n = height // BLK
    tile_blocks = n // 2
    tile = lanes // 2
    shape = (BLK, lanes)

    def get(f, i):
        r = pl.ds(pl.multiple_of(i * BLK, BLK), BLK)
        if f <= QY:
            return w_ref[f, r, :]
        if f == Z:
            return z_ref[r, :]
        if f == LR:
            return lr_ref[r, :]
        return c_ref[f - CH, r, :]

    def wet(i):
        lane = lax.broadcasted_iota(jnp.int32, shape, 1)
        row = i // tile_blocks
        return jnp.where(lane < tile, wet_ref[row, 0], wet_ref[row, 1]) > 0

    def put_grad(r, second, first):
        if first is None:
            g_ref[r, :] = second
        else:
            g_ref[r, :] += first

    gradient_passes(get, wet, n, lanes, scr, put_grad)
    for f in range(NF - 1):
        rs_ref[f, 0:8, :] = get(f, 0)
        rs_ref[f, 8:16, :] = get(f, n - 1)
        if f <= QY:
            ref = w_ref.at[f]
        elif f == Z:
            ref = z_ref
        elif f == LR:
            ref = lr_ref
        else:
            ref = c_ref.at[f - CH]
        lane = lax.broadcasted_iota(jnp.int32, (height, 128), 1)
        both = jnp.where(lane < 64, ref[:, 0:128], ref[:, lanes - 128 : lanes])
        turned = both.T
        tl_ref[f] = turned[0:8, :]
        tr_ref[f] = turned[120:128, :]
    rs_ref[WET, 0:8, :] = wet_rows(wet_ref, 0, shape, tile)
    rs_ref[WET, 8:16, :] = wet_rows(wet_ref, 1, shape, tile)
    lane = lax.broadcasted_iota(jnp.int32, (8, height), 1)

    def wet_cols(col):
        top = (wet_ref[0, col] > 0).astype(jnp.float32)
        bottom = (wet_ref[1, col] > 0).astype(jnp.float32)
        return jnp.where(lane < height // 2, top, bottom)

    tl_ref[WET] = wet_cols(0)
    tr_ref[WET] = wet_cols(1)


def pack_cols_kernel(ya_ref, yb_ref, tl_ref, tr_ref, a_ref, b_ref, pl_ref, pr_ref, k_scr):
    gx, nx = place("gx")
    gy, _ = place("gy")
    even_y = gy % 2 == 0
    lanes = ya_ref.shape[1]
    below = jnp.where(even_y, ya_ref[...], yb_ref[...])
    above = jnp.where(even_y, yb_ref[...], ya_ref[...])
    lane = lax.broadcasted_iota(jnp.int32, (above.shape[0], 128), 1)
    above = jnp.where(lane < 64, above[:, 0:128], above[:, lanes - 128 : lanes])
    below = jnp.where(lane < 64, below[:, 0:128], below[:, lanes - 128 : lanes])
    k_scr[...] = jnp.zeros_like(k_scr)
    for f in range(NF):
        k_scr[6 * f : 6 * f + 3, :] = above[3 * f : 3 * f + 3, :]
        k_scr[6 * f + 3 : 6 * f + 6, :] = below[3 * f : 3 * f + 3, :]
    turned = k_scr[...].T
    left_corner, right_corner = turned[0:8, :], turned[120:128, :]
    pl_ref[...] = left_corner
    pr_ref[...] = right_corner
    even = gx % 2 == 0
    a_ref[...] = jnp.zeros_like(a_ref)
    b_ref[...] = jnp.zeros_like(b_ref)
    first, last = gx == 0, gx == nx - 1
    for f in range(NF):
        sign = -1.0 if f in (QX, CX) else 1.0
        t = three_rows(tl_ref[f], 0, first, sign)
        b = three_rows(tr_ref[f], 5, last, sign)
        a_ref[3 * f : 3 * f + 3, :] = jnp.where(even, b, t)
        b_ref[3 * f : 3 * f + 3, :] = jnp.where(even, t, b)
    lane = lax.broadcasted_iota(jnp.int32, (3, 128), 1)
    flip = ((lane >= 6 * QX) & (lane < 6 * QX + 6)) | ((lane >= 6 * CX) & (lane < 6 * CX + 6))
    sign = jnp.where(flip, -1.0, 1.0)
    t = three_rows(left_corner, 0, first, sign)
    b = three_rows(right_corner, 5, last, sign)
    a_ref[32:35, 0:128] = jnp.where(even, b, t)
    b_ref[32:35, 0:128] = jnp.where(even, t, b)


def strip_gradient(s_ref, scr, g_ref):
    n = s_ref.shape[1] // BLK

    def get(f, i):
        return s_ref[f, pl.ds(pl.multiple_of(i * BLK, BLK), BLK), :]

    def put_grad(r, second, first):
        if first is None:
            g_ref[r, :] = second
        else:
            g_ref[r, :] += first

    gradient_passes(get, lambda i: get(WET, i) > 0.5, n, s_ref.shape[2], scr, put_grad)


def arctan_ratio(y, x):
    a = jnp.abs(y)
    big, small = jnp.maximum(a, x), jnp.minimum(a, x)
    far = small > 0.41421356 * big
    t = jnp.where(far, small - big, small) / jnp.where(far, small + big, big)
    z = t * t
    p = ((8.05374449538e-2 * z - 1.38776856032e-1) * z + 1.99777106478e-1) * z - 3.33329491539e-1
    r = p * z * t + t + jnp.where(far, math.pi / 4, 0.0)
    r = jnp.where(a > x, math.pi / 2 - r, r)
    return jnp.where(y < 0, -r, r)


def rim_kernel(
    ya_ref, yb_ref, xa_ref, xb_ref, rs_ref, tl_ref, tr_ref, pl_ref, pr_ref, g_ref, lr_ref, m_ref, v_ref,
    nr_ref, nm_ref, nv_ref, row_s, col_s, row_scr, col_scr, row_g, col_g, turn_scr, side_scr,
):
    gx, nx = place("gx")
    gy, _ = place("gy")
    even_x, even_y = gx % 2 == 0, gy % 2 == 0
    height, lanes = lr_ref.shape
    for f in range(NF):
        r = slice(3 * f, 3 * f + 3)
        ya, yb = ya_ref[r, :], yb_ref[r, :]
        row_s[f, 0:8, :] = jnp.ones((8, lanes), jnp.float32)
        row_s[f, 24:32, :] = jnp.ones((8, lanes), jnp.float32)
        row_s[f, 5:8, :] = jnp.where(even_y, yb, ya)
        row_s[f, 24:27, :] = jnp.where(even_y, ya, yb)
        row_s[f, 8:24, :] = rs_ref[f]
    strip_gradient(row_s, row_scr, row_g)
    left_in = jnp.where(even_x, xb_ref[...], xa_ref[...])
    right_in = jnp.where(even_x, xa_ref[...], xb_ref[...])
    for f, t in enumerate(TURNED):
        shift = (125 - 6 * f) % 128
        r = slice(3 * f, 3 * f + 3)
        col_s[t, 0:8, :] = jnp.ones((8, col_s.shape[2]), jnp.float32)
        col_s[t, 24:32, :] = jnp.ones((8, col_s.shape[2]), jnp.float32)
        col_s[t, 5:8, 0:height] = left_in[r, :]
        col_s[t, 24:27, 0:height] = right_in[r, :]
        col_s[t, 8:16, 0:height] = tl_ref[f]
        col_s[t, 16:24, 0:height] = tr_ref[f]
        far = slice(height, height + 128)
        col_s[t, 5:8, far] = pltpu.roll(left_in[32:40, 0:128], shift, 1)[0:3, :]
        col_s[t, 24:27, far] = pltpu.roll(right_in[32:40, 0:128], shift, 1)[0:3, :]
        col_s[t, 8:16, far] = pltpu.roll(pl_ref[...], shift, 1)
        col_s[t, 16:24, far] = pltpu.roll(pr_ref[...], shift, 1)
    strip_gradient(col_s, col_scr, col_g)
    turn_scr[...] = jnp.zeros_like(turn_scr)
    turn_scr[0:8, :] = col_g[8:16, 0:height]
    turn_scr[120:128, :] = col_g[16:24, 0:height]
    side_scr[...] = turn_scr[...].T
    lane = lax.broadcasted_iota(jnp.int32, (16, lanes), 1)
    beside = (lane < 3) | (lane >= lanes - 3)

    def update(r, rim):
        g = rim(g_ref[r, :])
        side = side_scr[r, :]
        g = jnp.where(beside, jnp.concatenate([side] * (lanes // 128), 1), g)
        nm = BETA_ONE * m_ref[r, :] + (1.0 - BETA_ONE) * g
        nv = BETA_TWO * v_ref[r, :] + (1.0 - BETA_TWO) * g * g
        nm_ref[r, :] = nm
        nv_ref[r, :] = nv
        root = jnp.sqrt(nv * (1.0 / (1.0 - BETA_TWO**UPDATES)))
        turn = arctan_ratio(nm * (1.0 / (1.0 - BETA_ONE**UPDATES)), root)
        nr_ref[r, :] = lr_ref[r, :] - (LEARN_RATE * ATAN_SCALE) * turn

    def inside(i, carry):
        update(pl.ds(pl.multiple_of(i * 16, 16), 16), lambda g: g)
        return carry

    row = lax.broadcasted_iota(jnp.int32, (16, lanes), 0)
    update(slice(0, 16), lambda g: jnp.where(row < 3, row_g[8:24, :], g))
    lax.fori_loop(1, height // 16 - 1, inside, 0)
    update(slice(height - 16, height), lambda g: jnp.where(row >= 13, row_g[8:24, :], g))


def swap_pairs(n, odd):
    pairs = []
    for i in range(n):
        j = i ^ 1 if not odd else ((i + 1) ^ 1) - 1
        pairs.append((i, j if 0 <= j < n else i))
    return pairs


def call(kernel, out_shapes, scratch=(), in_specs=None, flops=0, name=None):
    params = pltpu.CompilerParams(vmem_limit_bytes=VMEM_MB << 20)
    shapes = [jax.ShapeDtypeStruct(s, jnp.float32) for s in out_shapes]
    kwargs = {} if in_specs is None else {"in_specs": in_specs}
    return pl.pallas_call(
        kernel,
        out_shape=shapes,
        scratch_shapes=list(scratch),
        compiler_params=params,
        cost_estimate=pl.CostEstimate(flops=flops, bytes_accessed=flops // 8, transcendentals=0),
        name=name,
        **kwargs,
    )


def on_device(water, ground, rough, moment, second, wet_tiles, cot):
    height, lanes = ground.shape
    smem = pl.BlockSpec(memory_space=pltpu.SMEM)
    whole = pl.BlockSpec(memory_space=pltpu.VMEM)
    last = height // 8 - 1
    top3 = pl.BlockSpec((3, 8, lanes), lambda i: (0, 0, 0))
    bot3 = pl.BlockSpec((3, 8, lanes), lambda i: (0, last, 0))
    top1 = pl.BlockSpec((8, lanes), lambda i: (0, 0))
    bot1 = pl.BlockSpec((8, lanes), lambda i: (last, 0))
    pay = jax.ShapeDtypeStruct((32, lanes), jnp.float32)
    pay_spec = pl.BlockSpec((32, lanes), lambda i: (0, 0))
    y_a, y_b = pl.pallas_call(
        pack_rows_kernel,
        grid=(1,),
        in_specs=[smem, top3, bot3, top1, bot1, top1, bot1, top3, bot3],
        out_specs=[pay_spec, pay_spec],
        out_shape=[pay, pay],
        compiler_params=pltpu.CompilerParams(vmem_limit_bytes=VMEM_MB << 20),
        name="pack_rows",
    )(wet_tiles, water, water, ground, ground, rough, rough, cot, cot)
    ny, nx = lax.axis_size("gy"), lax.axis_size("gx")
    y_a = lax.ppermute(y_a, "gy", swap_pairs(ny, False))
    y_b = lax.ppermute(y_b, "gy", swap_pairs(ny, True))
    grad, row_own, col_left, col_right = call(
        inner_kernel,
        [(height, lanes), (NF, 16, lanes), (NF, 8, height), (NF, 8, height)],
        scratch=[pltpu.VMEM((10, height, lanes), jnp.float32)],
        in_specs=[smem, whole, whole, whole, whole],
        flops=20_000_000,
        name="inner",
    )(wet_tiles, water, ground, rough, cot)
    x_a, x_b, corner_left, corner_right = call(
        pack_cols_kernel,
        [(40, height), (40, height), (8, 128), (8, 128)],
        scratch=[pltpu.VMEM((128, 128), jnp.float32)],
        name="pack_cols",
    )(y_a, y_b, col_left, col_right)
    x_a = lax.ppermute(x_a, "gx", swap_pairs(nx, False))
    x_b = lax.ppermute(x_b, "gx", swap_pairs(nx, True))
    return tuple(
        call(
            rim_kernel,
            [(height, lanes)] * 3,
            scratch=[
                pltpu.VMEM((NF, 32, lanes), jnp.float32),
                pltpu.VMEM((NF, 32, height + 128), jnp.float32),
                pltpu.VMEM((10, 32, lanes), jnp.float32),
                pltpu.VMEM((10, 32, height + 128), jnp.float32),
                pltpu.VMEM((32, lanes), jnp.float32),
                pltpu.VMEM((32, height + 128), jnp.float32),
                pltpu.VMEM((128, height), jnp.float32),
                pltpu.VMEM((height, 128), jnp.float32),
            ],
            name="rim",
        )(
            y_a, y_b, x_a, x_b, row_own, col_left, col_right, corner_left, corner_right,
            grad, rough, moment, second,
        )
    )


def solution(mesh):
    flat = P("gy", "gx")
    deep = P(None, "gy", "gx")
    return jax.shard_map(
        on_device,
        mesh=mesh,
        in_specs=(deep, flat, flat, flat, flat, flat, deep),
        out_specs=(flat, flat, flat),
        check_vma=False,
    )
```

```python
import functools
import math

import jax
import jax.numpy as jnp
from jax import lax
from jax.experimental import pallas as pl
from jax.experimental.pallas import tpu as pltpu
from jax.sharding import PartitionSpec as P

UPDATES = 20
GRAVITY = 9.81
HALF_STEP = 0.05
LOG_DRAG = math.log(9.81)
SPEED_EPS = 0.0001
BETA_ONE = 0.9
BETA_TWO = 0.999
LEARN_RATE = 0.05
ATAN_SCALE = 1.27
H, QX, QY, Z, LR, CH, CX, CY, WET = range(9)
NF = 9
TURNED = (H, QY, QX, Z, LR, CH, CY, CX, WET)
BLK = 8
UNROLL = 8
VMEM_MB = 12


def from_prev_col(x):
    return pltpu.roll(x, 1, 1)


def from_next_col(x):
    return pltpu.roll(x, x.shape[1] - 1, 1)


def flux_parts(h, qx, qy, slope_x, slope_y):
    inv = 1.0 / h
    u, v = qx * inv, qy * inv
    press = (0.5 * GRAVITY) * h * h
    k = HALF_STEP
    fx1, fy1 = k * qx, k * qy
    fx2, fxy, fy3 = k * (qx * u + press), k * (qx * v), k * (qy * v + press)
    h4, x4, y4 = 0.25 * h, 0.25 * qx, 0.25 * qy
    cols = [
        from_prev_col(h4 + fx1) + from_next_col(h4 - fx1),
        from_prev_col(x4 + fx2) + from_next_col(x4 - fx2) - h * slope_x,
        from_prev_col(y4 + fxy) + from_next_col(y4 - fxy) - h * slope_y,
    ]
    down = [h4 + fy1, x4 + fxy, y4 + fy3]
    up = [h4 - fy1, x4 - fxy, y4 - fy3]
    return cols, down, up, u, v


def drag_parts(h, qx, qy, rough):
    s2 = qx * qx + qy * qy + SPEED_EPS
    rs = lax.rsqrt(s2)
    b = jnp.exp(2.0 * rough + LOG_DRAG - (7.0 / 3.0) * jnp.log(h)) * (s2 * rs)
    w = 1.0 / (1.0 + b)
    return b, w, rs * rs


def rows(j):
    if isinstance(j, int):
        return slice(j * BLK, j * BLK + BLK)
    return pl.ds(pl.multiple_of(j * BLK, BLK), BLK)


def take(ref, j, off=0):
    r = pl.ds(j * BLK + 8 + off, BLK)
    if off == 0 and not isinstance(j, int):
        r = pl.ds(pl.multiple_of(j * BLK + 8, 8), BLK)
    return jnp.concatenate([ref[t, r, :] for t in range(ref.shape[0])], 1)


def give(ref, j, value):
    put(ref, pl.ds(pl.multiple_of(j * BLK + 8, 8), BLK), value)


def put(ref, r, value, at=0):
    for t in range(value.shape[1] // 128):
        ref[at + t, r, :] = value[:, 128 * t : 128 * t + 128]


def looped(n, step):
    if n <= 8:
        for j in range(n):
            step(j)
        return

    def body(j, carry):
        step(j)
        return carry

    lax.fori_loop(0, n, body, 0, unroll=UNROLL)


UH, UX, UY, SX, SY, GA, GB = range(7)
N_AHEAD, N_ACROSS, N_SHIFTED = 7, 6, 9
DOWN, UP, ZS = 0, 3, 6
PH, PX, PY = range(3)
ADJ = 6
VU, VV, PG = 3, 4, 5


def gathered(shifted, across, j):
    r = rows(j)
    return [
        take(shifted.at[DOWN + f], j, -1) + take(shifted.at[UP + f], j, 1) + across[f, r, :]
        for f in range(3)
    ]


def first_pass(get, wet, n, scr, shifted, across):
    looped(n, lambda j: give(shifted.at[ZS], j, get(Z, j)))

    def parts(j):
        r = rows(j)
        kg = HALF_STEP * GRAVITY
        z = get(Z, j)
        sx = kg * (from_next_col(z) - from_prev_col(z))
        sy = kg * (take(shifted.at[ZS], j, 1) - take(shifted.at[ZS], j, -1))
        scr[SX, r, :] = sx
        scr[SY, r, :] = sy
        cols, down, up, _, _ = flux_parts(get(H, j), get(QX, j), get(QY, j), sx, sy)
        for f in range(3):
            across[f, r, :] = cols[f]
            give(shifted.at[DOWN + f], j, down[f])
            give(shifted.at[UP + f], j, up[f])

    looped(n, parts)

    def finish(j):
        r = rows(j)
        h, qx, qy = gathered(shifted, across, j)
        b, w, _ = drag_parts(h, qx, qy, get(LR, j))
        m = wet(j)
        scr[UH, r, :] = jnp.where(m, h, get(H, j))
        scr[UX, r, :] = jnp.where(m, qx * w, get(QX, j))
        scr[UY, r, :] = jnp.where(m, qy * w, get(QY, j))
        t = jnp.where(m, -2.0 * b * w * w, 0.0)
        scr[GA, r, :] = t * qx
        scr[GB, r, :] = t * qy

    looped(n, finish)


def last_passes(get, wet, n, scr, shifted, across, put_grad):
    def parts(j):
        r = rows(j)
        cols, down, up, u, v = flux_parts(*(scr[f, r, :] for f in (UH, UX, UY, SX, SY)))
        across[VU, r, :] = u
        across[VV, r, :] = v
        for f in range(3):
            across[f, r, :] = cols[f]
            give(shifted.at[DOWN + f], j, down[f])
            give(shifted.at[UP + f], j, up[f])

    looped(n, parts)

    def finish(j):
        h, qx, qy = gathered(shifted, across, j)
        b, w, inv_s2 = drag_parts(h, qx, qy, get(LR, j))
        m = wet(j)
        ch, cx, cy = get(CH, j), get(CX, j), get(CY, j)
        t = (cx * qx + cy * qy) * (w * w) * b
        ts = t * inv_s2
        return [
            jnp.where(m, ch + (7.0 / 3.0) * t / h, 0.0),
            jnp.where(m, cx * w - ts * qx, 0.0),
            jnp.where(m, cy * w - ts * qy, 0.0),
            jnp.where(m, -2.0 * t, 0.0),
        ]

    def finish_all(j):
        for f, value in enumerate(finish(j)):
            if f < 3:
                give(shifted.at[ADJ + f], j, value)
            else:
                across[PG, rows(j), :] = value

    looped(n, finish_all)

    def back(j):
        r = rows(j)

        def four(f):
            ref = shifted.at[ADJ + f]
            cur = take(ref, j)
            return from_next_col(cur), from_prev_col(cur), take(ref, j, 1), take(ref, j, -1)

        he, hw, hs, hn = four(PH)
        xe, xw, xs, xn = four(PX)
        ye, yw, ys, yn = four(PY)
        u, v = across[VU, r, :], across[VV, r, :]
        k = HALF_STEP
        cross = k * ((ye - yw) + (xs - xn))
        cot_x = (
            0.25 * ((xe + xw) + (xs + xn))
            + k * (he - hw)
            + (2.0 * k) * u * (xe - xw)
            + v * cross
        )
        cot_y = (
            0.25 * ((ye + yw) + (ys + yn))
            + k * (hs - hn)
            + (2.0 * k) * v * (ys - yn)
            + u * cross
        )
        put_grad(j, across[PG, r, :] + scr[GA, r, :] * cot_x + scr[GB, r, :] * cot_y)

    looped(n, back)


def place(axis):
    index = lax.axis_index(axis)
    return index, lax.axis_size(axis)


def three_rows(block, first, mirrored, sign):
    natural = block[first : first + 3, :]
    reverse = jnp.concatenate([block[first + 2 - d : first + 3 - d, :] for d in range(3)], 0)
    return jnp.where(mirrored, sign * reverse, natural)


def pack_rows_kernel(wet_hbm, w_hbm, z_hbm, lr_hbm, c_hbm, a_ref, b_ref, wet_ref, wet_s, top, bot, sems):
    height, lanes = z_hbm.shape
    copies = [pltpu.make_async_copy(wet_hbm, wet_s, sems.at[0])]
    for side, (buf, row) in enumerate(((top, 0), (bot, height - 8))):
        r = pl.ds(row, 8)
        for at, (src, dst) in enumerate((
            (w_hbm.at[:, r, :], buf.at[pl.ds(0, 3)]),
            (z_hbm.at[r, :], buf.at[Z]),
            (lr_hbm.at[r, :], buf.at[LR]),
            (c_hbm.at[:, r, :], buf.at[pl.ds(CH, 3)]),
        )):
            copies.append(pltpu.make_async_copy(src, dst, sems.at[1 + 4 * side + at]))
    for copy in copies:
        copy.start()
    gy, ny = place("gy")
    even = gy % 2 == 0
    lane = lax.broadcasted_iota(jnp.int32, (8, lanes), 1)
    a_ref[24:32, :] = jnp.zeros((8, lanes), jnp.float32)
    b_ref[24:32, :] = jnp.zeros((8, lanes), jnp.float32)
    for copy in copies:
        copy.wait()
    for row in range(2):
        left = (wet_s[row, 0] > 0).astype(jnp.float32)
        right = (wet_s[row, 1] > 0).astype(jnp.float32)
        wet_ref[8 * row : 8 * row + 8, :] = jnp.where(lane < lanes // 2, left, right)
    for f in range(NF):
        sign = -1.0 if f in (QY, CY) else 1.0
        t = three_rows(top[f] if f < WET else wet_ref[0:8, :], 0, gy == 0, sign)
        b = three_rows(bot[f] if f < WET else wet_ref[8:16, :], 5, gy == ny - 1, sign)
        a_ref[3 * f : 3 * f + 3, :] = jnp.where(even, b, t)
        b_ref[3 * f : 3 * f + 3, :] = jnp.where(even, t, b)


def tile_wet(wet_ref, j, n):
    return wet_ref[rows(j // (n // 2)), :] > 0.5


def forward_kernel(wet_ref, w_ref, z_ref, lr_ref, c_ref, scr, rs_ref, tl_ref, tr_ref, shifted, across):
    height, lanes = z_ref.shape
    n = height // BLK

    def field(f):
        if f <= QY:
            return w_ref.at[f]
        return z_ref if f == Z else lr_ref if f == LR else c_ref.at[f - CH]

    def get(f, j):
        return field(f)[rows(j), :]

    first_pass(get, lambda j: tile_wet(wet_ref, j, n), n, scr, shifted, across)
    lane = lax.broadcasted_iota(jnp.int32, (height, 128), 1)
    for f in range(WET):
        ref = field(f)
        rs_ref[f, 0:8, :] = ref[0:8, :]
        rs_ref[f, 8:16, :] = ref[height - 8 : height, :]
        turned = jnp.where(lane < 64, ref[:, 0:128], ref[:, lanes - 128 : lanes]).T
        tl_ref[f] = turned[0:8, :]
        tr_ref[f] = turned[120:128, :]
    top, bottom = wet_ref[0:8, :], wet_ref[8:16, :]
    rs_ref[WET, 0:8, :] = top
    rs_ref[WET, 8:16, :] = bottom
    half = lanes // 2
    tl_ref[WET] = jnp.concatenate([top[:, :half], bottom[:, :half]], 1)
    tr_ref[WET] = jnp.concatenate([top[:, half:], bottom[:, half:]], 1)


def backward_kernel(after_ref, wet_ref, lr_ref, c_ref, scr, g_ref, shifted, across):
    n = lr_ref.shape[0] // BLK

    def get(f, j):
        return (lr_ref if f == LR else c_ref.at[f - CH])[rows(j), :]

    def put_grad(j, value):
        g_ref[rows(j), :] = value

    last_passes(get, lambda j: tile_wet(wet_ref, j, n), n, scr, shifted, across, put_grad)


def pack_cols_kernel(ya_ref, yb_ref, tl_ref, tr_ref, a_ref, b_ref, pl_ref, pr_ref, k_scr):
    gx, nx = place("gx")
    gy, _ = place("gy")
    even_y = gy % 2 == 0
    lanes = ya_ref.shape[1]
    below = jnp.where(even_y, ya_ref[...], yb_ref[...])
    above = jnp.where(even_y, yb_ref[...], ya_ref[...])
    lane = lax.broadcasted_iota(jnp.int32, (above.shape[0], 128), 1)
    above = jnp.where(lane < 64, above[:, 0:128], above[:, lanes - 128 : lanes])
    below = jnp.where(lane < 64, below[:, 0:128], below[:, lanes - 128 : lanes])
    k_scr[...] = jnp.zeros_like(k_scr)
    for f in range(NF):
        k_scr[6 * f : 6 * f + 3, :] = above[3 * f : 3 * f + 3, :]
        k_scr[6 * f + 3 : 6 * f + 6, :] = below[3 * f : 3 * f + 3, :]
    turned = k_scr[...].T
    left_corner, right_corner = turned[0:8, :], turned[120:128, :]
    pl_ref[...] = left_corner
    pr_ref[...] = right_corner
    even = gx % 2 == 0
    a_ref[...] = jnp.zeros_like(a_ref)
    b_ref[...] = jnp.zeros_like(b_ref)
    first, last = gx == 0, gx == nx - 1
    for f in range(NF):
        sign = -1.0 if f in (QX, CX) else 1.0
        t = three_rows(tl_ref[f], 0, first, sign)
        b = three_rows(tr_ref[f], 5, last, sign)
        a_ref[3 * f : 3 * f + 3, :] = jnp.where(even, b, t)
        b_ref[3 * f : 3 * f + 3, :] = jnp.where(even, t, b)
    lane = lax.broadcasted_iota(jnp.int32, (3, 128), 1)
    flip = ((lane >= 6 * QX) & (lane < 6 * QX + 6)) | ((lane >= 6 * CX) & (lane < 6 * CX + 6))
    sign = jnp.where(flip, -1.0, 1.0)
    t = three_rows(left_corner, 0, first, sign)
    b = three_rows(right_corner, 5, last, sign)
    a_ref[32:35, 0:128] = jnp.where(even, b, t)
    b_ref[32:35, 0:128] = jnp.where(even, t, b)


def strip_gradient(s_ref, scr, shifted, across, g_ref):
    n = s_ref.shape[1] // BLK

    def get(f, j):
        return s_ref[f, rows(j), :]

    def wet(j):
        return get(WET, j) > 0.5

    def put_grad(j, value):
        g_ref[rows(j), :] = value

    first_pass(get, wet, n, scr, shifted, across)
    last_passes(get, wet, n, scr, shifted, across, put_grad)


def arctan_ratio(y, x):
    a = jnp.abs(y)
    big, small = jnp.maximum(a, x), jnp.minimum(a, x)
    far = small > 0.41421356 * big
    t = jnp.where(far, small - big, small) / jnp.where(far, small + big, big)
    z = t * t
    p = ((8.05374449538e-2 * z - 1.38776856032e-1) * z + 1.99777106478e-1) * z - 3.33329491539e-1
    r = p * z * t + t + jnp.where(far, math.pi / 4, 0.0)
    r = jnp.where(a > x, math.pi / 2 - r, r)
    return jnp.where(y < 0, -r, r)


def rim_kernel(
    ya_ref, yb_ref, xa_ref, xb_ref, rs_ref, tl_ref, tr_ref, pl_ref, pr_ref, g_ref, lr_ref, m_ref, v_ref,
    nr_ref, nm_ref, nv_ref, row_s, col_s, row_scr, col_scr, row_sh, col_sh, row_ac, col_ac, row_g, col_g, turn_scr, side_scr,
):
    gx, nx = place("gx")
    gy, _ = place("gy")
    even_x, even_y = gx % 2 == 0, gy % 2 == 0
    height, lanes = lr_ref.shape
    for f in range(NF):
        r = slice(3 * f, 3 * f + 3)
        ya, yb = ya_ref[r, :], yb_ref[r, :]
        row_s[f, 0:8, :] = jnp.ones((8, lanes), jnp.float32)
        row_s[f, 24:32, :] = jnp.ones((8, lanes), jnp.float32)
        row_s[f, 5:8, :] = jnp.where(even_y, yb, ya)
        row_s[f, 24:27, :] = jnp.where(even_y, ya, yb)
        row_s[f, 8:24, :] = rs_ref[f]
    strip_gradient(row_s, row_scr, row_sh, row_ac, row_g)
    left_in = jnp.where(even_x, xb_ref[...], xa_ref[...])
    right_in = jnp.where(even_x, xa_ref[...], xb_ref[...])
    for f, t in enumerate(TURNED):
        shift = (125 - 6 * f) % 128
        r = slice(3 * f, 3 * f + 3)
        col_s[t, 0:8, :] = jnp.ones((8, height + 128), jnp.float32)
        col_s[t, 24:32, :] = jnp.ones((8, height + 128), jnp.float32)
        col_s[t, 5:8, 0:height] = left_in[r, :]
        col_s[t, 24:27, 0:height] = right_in[r, :]
        col_s[t, 8:16, 0:height] = tl_ref[f]
        col_s[t, 16:24, 0:height] = tr_ref[f]
        col_s[t, 5:8, height:] = pltpu.roll(left_in[32:40, 0:128], shift, 1)[0:3, :]
        col_s[t, 24:27, height:] = pltpu.roll(right_in[32:40, 0:128], shift, 1)[0:3, :]
        col_s[t, 8:16, height:] = pltpu.roll(pl_ref[...], shift, 1)
        col_s[t, 16:24, height:] = pltpu.roll(pr_ref[...], shift, 1)
    strip_gradient(col_s, col_scr, col_sh, col_ac, col_g)
    turn_scr[...] = jnp.zeros_like(turn_scr)
    turn_scr[0:8, :] = col_g[8:16, 0:height]
    turn_scr[120:128, :] = col_g[16:24, 0:height]
    side_scr[...] = turn_scr[...].T
    lane = lax.broadcasted_iota(jnp.int32, (16, lanes), 1)
    beside = (lane < 3) | (lane >= lanes - 3)

    def update(r, rim):
        g = rim(g_ref[r, :])
        side = side_scr[r, :]
        g = jnp.where(beside, jnp.concatenate([side] * (lanes // 128), 1), g)
        nm = BETA_ONE * m_ref[r, :] + (1.0 - BETA_ONE) * g
        nv = BETA_TWO * v_ref[r, :] + (1.0 - BETA_TWO) * g * g
        nm_ref[r, :] = nm
        nv_ref[r, :] = nv
        root = jnp.sqrt(nv * (1.0 / (1.0 - BETA_TWO**UPDATES)))
        turn = arctan_ratio(nm * (1.0 / (1.0 - BETA_ONE**UPDATES)), root)
        nr_ref[r, :] = lr_ref[r, :] - (LEARN_RATE * ATAN_SCALE) * turn

    def inside(i, carry):
        update(pl.ds(pl.multiple_of(i * 16, 16), 16), lambda g: g)
        return carry

    row = lax.broadcasted_iota(jnp.int32, (16, lanes), 0)
    update(slice(0, 16), lambda g: jnp.where(row < 3, row_g[8:24, :], g))
    lax.fori_loop(1, height // 16 - 1, inside, 0)
    update(slice(height - 16, height), lambda g: jnp.where(row >= 13, row_g[8:24, :], g))


def swap_pairs(n, odd):
    pairs = []
    for i in range(n):
        j = i ^ 1 if not odd else ((i + 1) ^ 1) - 1
        pairs.append((i, j if 0 <= j < n else i))
    return pairs


def call(kernel, out_shapes, scratch=(), in_specs=None, flops=0, name=None, vmem_mb=VMEM_MB):
    params = pltpu.CompilerParams(vmem_limit_bytes=vmem_mb << 20)
    shapes = [jax.ShapeDtypeStruct(s, jnp.float32) for s in out_shapes]
    kwargs = {} if in_specs is None else {"in_specs": in_specs}
    return pl.pallas_call(
        kernel,
        out_shape=shapes,
        scratch_shapes=list(scratch),
        compiler_params=params,
        cost_estimate=pl.CostEstimate(flops=flops, bytes_accessed=flops // 8, transcendentals=0),
        name=name,
        **kwargs,
    )


def on_device(water, ground, rough, moment, second, wet_tiles, cot):
    height, lanes = ground.shape
    hbm = pl.BlockSpec(memory_space=pltpu.HBM)
    y_a, y_b, wet = call(
        pack_rows_kernel,
        [(32, lanes), (32, lanes), (16, lanes)],
        scratch=[
            pltpu.SMEM((2, 2), jnp.int32),
            pltpu.VMEM((8, 8, lanes), jnp.float32),
            pltpu.VMEM((8, 8, lanes), jnp.float32),
            pltpu.SemaphoreType.DMA((9,)),
        ],
        in_specs=[hbm] * 5,
        name="pack_rows",
        vmem_mb=60,
    )(wet_tiles, water, ground, rough, cot)
    ny, nx = lax.axis_size("gy"), lax.axis_size("gx")
    y_a = lax.ppermute(y_a, "gy", swap_pairs(ny, False))
    y_b = lax.ppermute(y_b, "gy", swap_pairs(ny, True))
    scratch = [
        pltpu.VMEM((N_SHIFTED, lanes // 128, height + 16, 128), jnp.float32),
        pltpu.VMEM((N_ACROSS, height, lanes), jnp.float32),
    ]
    ahead, row_own, col_left, col_right = call(
        forward_kernel,
        [(N_AHEAD, height, lanes), (NF, 16, lanes), (NF, 8, height), (NF, 8, height)],
        scratch=scratch,
        flops=20_000_000,
        name="forward",
    )(wet, water, ground, rough, cot)
    x_a, x_b, corner_left, corner_right = call(
        pack_cols_kernel,
        [(40, height), (40, height), (8, 128), (8, 128)],
        scratch=[pltpu.VMEM((128, 128), jnp.float32)],
        name="pack_cols",
    )(y_a, y_b, col_left, col_right)
    (grad,) = call(
        backward_kernel,
        [(height, lanes)],
        scratch=scratch,
        flops=20_000_000,
        name="backward",
    )(corner_left, wet, rough, cot, ahead)
    x_a = lax.ppermute(x_a, "gx", swap_pairs(nx, False))
    x_b = lax.ppermute(x_b, "gx", swap_pairs(nx, True))
    return tuple(
        call(
            rim_kernel,
            [(height, lanes)] * 3,
            scratch=[
                pltpu.VMEM((NF, 32, lanes), jnp.float32),
                pltpu.VMEM((NF, 32, height + 128), jnp.float32),
                pltpu.VMEM((N_AHEAD, 32, lanes), jnp.float32),
                pltpu.VMEM((N_AHEAD, 32, height + 128), jnp.float32),
                pltpu.VMEM((N_SHIFTED, lanes // 128, 48, 128), jnp.float32),
                pltpu.VMEM((N_SHIFTED, height // 128 + 1, 48, 128), jnp.float32),
                pltpu.VMEM((N_ACROSS, 32, lanes), jnp.float32),
                pltpu.VMEM((N_ACROSS, 32, height + 128), jnp.float32),
                pltpu.VMEM((32, lanes), jnp.float32),
                pltpu.VMEM((32, height + 128), jnp.float32),
                pltpu.VMEM((128, height), jnp.float32),
                pltpu.VMEM((height, 128), jnp.float32),
            ],
            name="rim",
        )(
            y_a, y_b, x_a, x_b, row_own, col_left, col_right, corner_left, corner_right,
            grad, rough, moment, second,
        )
    )


def solution(mesh):
    flat = P("gy", "gx")
    deep = P(None, "gy", "gx")
    return jax.shard_map(
        on_device,
        mesh=mesh,
        in_specs=(deep, flat, flat, flat, flat, flat, deep),
        out_specs=(flat, flat, flat),
        check_vma=False,
    )
```

```python
import functools
import math

import jax
import jax.numpy as jnp
from jax import lax
from jax.experimental import pallas as pl
from jax.experimental.pallas import tpu as pltpu
from jax.sharding import PartitionSpec as P

UPDATES = 20
GRAVITY = 9.81
HALF_STEP = 0.05
LOG_DRAG = math.log(9.81)
SPEED_EPS = 0.0001
BETA_ONE = 0.9
BETA_TWO = 0.999
LEARN_RATE = 0.05
ATAN_SCALE = 1.27
H, QX, QY, Z, LR, CH, CX, CY, WET = range(9)
NF = 9
TURNED = (H, QY, QX, Z, LR, CH, CY, CX, WET)
BLK = 8
UNROLL = 8
VMEM_MB = 12


def from_prev_col(x):
    return pltpu.roll(x, 1, 1)


def from_next_col(x):
    return pltpu.roll(x, x.shape[1] - 1, 1)


def flux_parts(h, qx, qy, slope_x, slope_y):
    inv = 1.0 / h
    u, v = qx * inv, qy * inv
    press = (0.5 * GRAVITY) * h * h
    k = HALF_STEP
    fx1, fy1 = k * qx, k * qy
    fx2, fxy, fy3 = k * (qx * u + press), k * (qx * v), k * (qy * v + press)
    h4, x4, y4 = 0.25 * h, 0.25 * qx, 0.25 * qy
    cols = [
        from_prev_col(h4 + fx1) + from_next_col(h4 - fx1),
        from_prev_col(x4 + fx2) + from_next_col(x4 - fx2) - h * slope_x,
        from_prev_col(y4 + fxy) + from_next_col(y4 - fxy) - h * slope_y,
    ]
    down = [h4 + fy1, x4 + fxy, y4 + fy3]
    up = [h4 - fy1, x4 - fxy, y4 - fy3]
    return cols, down, up, u, v


def drag_parts(h, qx, qy, rough):
    s2 = qx * qx + qy * qy + SPEED_EPS
    rs = lax.rsqrt(s2)
    b = jnp.exp(2.0 * rough + LOG_DRAG - (7.0 / 3.0) * jnp.log(h)) * (s2 * rs)
    w = 1.0 / (1.0 + b)
    return b, w, rs * rs


def rows(j):
    if isinstance(j, int):
        return slice(j * BLK, j * BLK + BLK)
    return pl.ds(pl.multiple_of(j * BLK, BLK), BLK)


def take(ref, j, off=0):
    r = pl.ds(j * BLK + 8 + off, BLK)
    if off == 0 and not isinstance(j, int):
        r = pl.ds(pl.multiple_of(j * BLK + 8, 8), BLK)
    return jnp.concatenate([ref[t, r, :] for t in range(ref.shape[0])], 1)


def give(ref, j, value):
    put(ref, pl.ds(pl.multiple_of(j * BLK + 8, 8), BLK), value)


def put(ref, r, value, at=0):
    for t in range(value.shape[1] // 128):
        ref[at + t, r, :] = value[:, 128 * t : 128 * t + 128]


def looped(n, step):
    if n <= 8:
        for j in range(n):
            step(j)
        return

    def body(j, carry):
        step(j)
        return carry

    lax.fori_loop(0, n, body, 0, unroll=UNROLL)


UH, UX, UY, SX, SY, GA, GB = range(7)
N_AHEAD, N_ACROSS, N_SHIFTED = 7, 6, 9
DOWN, UP, ZS = 0, 3, 6
PH, PX, PY = range(3)
ADJ = 6
VU, VV, PG = 3, 4, 5


def gathered(shifted, across, j):
    r = rows(j)
    return [
        take(shifted.at[DOWN + f], j, -1) + take(shifted.at[UP + f], j, 1) + across[f, r, :]
        for f in range(3)
    ]


def first_pass(get, wet, n, scr, shifted, across):
    looped(n, lambda j: give(shifted.at[ZS], j, get(Z, j)))

    def parts(j):
        r = rows(j)
        kg = HALF_STEP * GRAVITY
        z = get(Z, j)
        sx = kg * (from_next_col(z) - from_prev_col(z))
        sy = kg * (take(shifted.at[ZS], j, 1) - take(shifted.at[ZS], j, -1))
        scr[SX, r, :] = sx
        scr[SY, r, :] = sy
        cols, down, up, _, _ = flux_parts(get(H, j), get(QX, j), get(QY, j), sx, sy)
        for f in range(3):
            across[f, r, :] = cols[f]
            give(shifted.at[DOWN + f], j, down[f])
            give(shifted.at[UP + f], j, up[f])

    looped(n, parts)

    def finish(j):
        r = rows(j)
        h, qx, qy = gathered(shifted, across, j)
        b, w, _ = drag_parts(h, qx, qy, get(LR, j))
        m = wet(j)
        scr[UH, r, :] = jnp.where(m, h, get(H, j))
        scr[UX, r, :] = jnp.where(m, qx * w, get(QX, j))
        scr[UY, r, :] = jnp.where(m, qy * w, get(QY, j))
        t = jnp.where(m, -2.0 * b * w * w, 0.0)
        scr[GA, r, :] = t * qx
        scr[GB, r, :] = t * qy

    looped(n, finish)


def last_passes(get, wet, n, scr, shifted, across, put_grad):
    def parts(j):
        r = rows(j)
        cols, down, up, u, v = flux_parts(*(scr[f, r, :] for f in (UH, UX, UY, SX, SY)))
        across[VU, r, :] = u
        across[VV, r, :] = v
        for f in range(3):
            across[f, r, :] = cols[f]
            give(shifted.at[DOWN + f], j, down[f])
            give(shifted.at[UP + f], j, up[f])

    looped(n, parts)

    def finish(j):
        h, qx, qy = gathered(shifted, across, j)
        b, w, inv_s2 = drag_parts(h, qx, qy, get(LR, j))
        m = wet(j)
        ch, cx, cy = get(CH, j), get(CX, j), get(CY, j)
        t = (cx * qx + cy * qy) * (w * w) * b
        ts = t * inv_s2
        return [
            jnp.where(m, ch + (7.0 / 3.0) * t / h, 0.0),
            jnp.where(m, cx * w - ts * qx, 0.0),
            jnp.where(m, cy * w - ts * qy, 0.0),
            jnp.where(m, -2.0 * t, 0.0),
        ]

    def finish_all(j):
        for f, value in enumerate(finish(j)):
            if f < 3:
                give(shifted.at[ADJ + f], j, value)
            else:
                across[PG, rows(j), :] = value

    looped(n, finish_all)

    def back(j):
        r = rows(j)

        def four(f):
            ref = shifted.at[ADJ + f]
            cur = take(ref, j)
            return from_next_col(cur), from_prev_col(cur), take(ref, j, 1), take(ref, j, -1)

        he, hw, hs, hn = four(PH)
        xe, xw, xs, xn = four(PX)
        ye, yw, ys, yn = four(PY)
        u, v = across[VU, r, :], across[VV, r, :]
        k = HALF_STEP
        cross = k * ((ye - yw) + (xs - xn))
        cot_x = (
            0.25 * ((xe + xw) + (xs + xn))
            + k * (he - hw)
            + (2.0 * k) * u * (xe - xw)
            + v * cross
        )
        cot_y = (
            0.25 * ((ye + yw) + (ys + yn))
            + k * (hs - hn)
            + (2.0 * k) * v * (ys - yn)
            + u * cross
        )
        put_grad(j, across[PG, r, :] + scr[GA, r, :] * cot_x + scr[GB, r, :] * cot_y)

    looped(n, back)


def place(axis):
    index = lax.axis_index(axis)
    return index, lax.axis_size(axis)


def three_rows(block, first, mirrored, sign):
    natural = block[first : first + 3, :]
    reverse = jnp.concatenate([block[first + 2 - d : first + 3 - d, :] for d in range(3)], 0)
    return jnp.where(mirrored, sign * reverse, natural)


def pack_rows_kernel(wet_hbm, w_hbm, z_hbm, lr_hbm, c_hbm, b_ref, a_ref, wet_ref, wet_s, top, bot, sems):
    height, lanes = z_hbm.shape
    copies = [pltpu.make_async_copy(wet_hbm, wet_s, sems.at[0])]
    for side, (buf, row) in enumerate(((top, 0), (bot, height - 8))):
        r = pl.ds(row, 8)
        for at, (src, dst) in enumerate((
            (w_hbm.at[:, r, :], buf.at[pl.ds(0, 3)]),
            (z_hbm.at[r, :], buf.at[Z]),
            (lr_hbm.at[r, :], buf.at[LR]),
            (c_hbm.at[:, r, :], buf.at[pl.ds(CH, 3)]),
        )):
            copies.append(pltpu.make_async_copy(src, dst, sems.at[1 + 4 * side + at]))
    for copy in copies:
        copy.start()
    gy, ny = place("gy")
    even = gy % 2 == 0
    lane = lax.broadcasted_iota(jnp.int32, (8, lanes), 1)
    a_ref[24:32, :] = jnp.zeros((8, lanes), jnp.float32)
    b_ref[24:32, :] = jnp.zeros((8, lanes), jnp.float32)
    for copy in copies:
        copy.wait()
    for row in range(2):
        left = (wet_s[row, 0] > 0).astype(jnp.float32)
        right = (wet_s[row, 1] > 0).astype(jnp.float32)
        wet_ref[8 * row : 8 * row + 8, :] = jnp.where(lane < lanes // 2, left, right)
    for f in range(NF):
        sign = -1.0 if f in (QY, CY) else 1.0
        t = three_rows(top[f] if f < WET else wet_ref[0:8, :], 0, gy == 0, sign)
        b = three_rows(bot[f] if f < WET else wet_ref[8:16, :], 5, gy == ny - 1, sign)
        a_ref[3 * f : 3 * f + 3, :] = jnp.where(even, b, t)
        b_ref[3 * f : 3 * f + 3, :] = jnp.where(even, t, b)


def tile_wet(wet_ref, j, n):
    return wet_ref[rows(j // (n // 2)), :] > 0.5


def forward_kernel(wet_ref, w_ref, z_ref, lr_ref, c_ref, scr, rs_ref, tl_ref, tr_ref, shifted, across):
    height, lanes = z_ref.shape
    n = height // BLK

    def field(f):
        if f <= QY:
            return w_ref.at[f]
        return z_ref if f == Z else lr_ref if f == LR else c_ref.at[f - CH]

    def get(f, j):
        return field(f)[rows(j), :]

    first_pass(get, lambda j: tile_wet(wet_ref, j, n), n, scr, shifted, across)
    lane = lax.broadcasted_iota(jnp.int32, (height, 128), 1)
    for f in range(WET):
        ref = field(f)
        rs_ref[f, 0:8, :] = ref[0:8, :]
        rs_ref[f, 8:16, :] = ref[height - 8 : height, :]
        turned = jnp.where(lane < 64, ref[:, 0:128], ref[:, lanes - 128 : lanes]).T
        tl_ref[f] = turned[0:8, :]
        tr_ref[f] = turned[120:128, :]
    top, bottom = wet_ref[0:8, :], wet_ref[8:16, :]
    rs_ref[WET, 0:8, :] = top
    rs_ref[WET, 8:16, :] = bottom
    half = lanes // 2
    tl_ref[WET] = jnp.concatenate([top[:, :half], bottom[:, :half]], 1)
    tr_ref[WET] = jnp.concatenate([top[:, half:], bottom[:, half:]], 1)


def backward_kernel(after_ref, wet_ref, lr_ref, c_ref, scr, g_ref, shifted, across):
    n = lr_ref.shape[0] // BLK

    def get(f, j):
        return (lr_ref if f == LR else c_ref.at[f - CH])[rows(j), :]

    def put_grad(j, value):
        g_ref[rows(j), :] = value

    last_passes(get, lambda j: tile_wet(wet_ref, j, n), n, scr, shifted, across, put_grad)


def pack_cols_kernel(yb_ref, ya_ref, tl_ref, tr_ref, b_ref, a_ref, pl_ref, pr_ref, k_scr):
    gx, nx = place("gx")
    gy, _ = place("gy")
    even_y = gy % 2 == 0
    lanes = ya_ref.shape[1]
    below = jnp.where(even_y, ya_ref[...], yb_ref[...])
    above = jnp.where(even_y, yb_ref[...], ya_ref[...])
    lane = lax.broadcasted_iota(jnp.int32, (above.shape[0], 128), 1)
    above = jnp.where(lane < 64, above[:, 0:128], above[:, lanes - 128 : lanes])
    below = jnp.where(lane < 64, below[:, 0:128], below[:, lanes - 128 : lanes])
    k_scr[...] = jnp.zeros_like(k_scr)
    for f in range(NF):
        k_scr[6 * f : 6 * f + 3, :] = above[3 * f : 3 * f + 3, :]
        k_scr[6 * f + 3 : 6 * f + 6, :] = below[3 * f : 3 * f + 3, :]
    turned = k_scr[...].T
    left_corner, right_corner = turned[0:8, :], turned[120:128, :]
    pl_ref[...] = left_corner
    pr_ref[...] = right_corner
    even = gx % 2 == 0
    a_ref[...] = jnp.zeros_like(a_ref)
    b_ref[...] = jnp.zeros_like(b_ref)
    first, last = gx == 0, gx == nx - 1
    for f in range(NF):
        sign = -1.0 if f in (QX, CX) else 1.0
        t = three_rows(tl_ref[f], 0, first, sign)
        b = three_rows(tr_ref[f], 5, last, sign)
        a_ref[3 * f : 3 * f + 3, :] = jnp.where(even, b, t)
        b_ref[3 * f : 3 * f + 3, :] = jnp.where(even, t, b)
    lane = lax.broadcasted_iota(jnp.int32, (3, 128), 1)
    flip = ((lane >= 6 * QX) & (lane < 6 * QX + 6)) | ((lane >= 6 * CX) & (lane < 6 * CX + 6))
    sign = jnp.where(flip, -1.0, 1.0)
    t = three_rows(left_corner, 0, first, sign)
    b = three_rows(right_corner, 5, last, sign)
    a_ref[32:35, 0:128] = jnp.where(even, b, t)
    b_ref[32:35, 0:128] = jnp.where(even, t, b)


def strip_gradient(s_ref, scr, shifted, across, g_ref):
    n = s_ref.shape[1] // BLK

    def get(f, j):
        return s_ref[f, rows(j), :]

    def wet(j):
        return get(WET, j) > 0.5

    def put_grad(j, value):
        g_ref[rows(j), :] = value

    first_pass(get, wet, n, scr, shifted, across)
    last_passes(get, wet, n, scr, shifted, across, put_grad)


def arctan_ratio(y, x):
    a = jnp.abs(y)
    big, small = jnp.maximum(a, x), jnp.minimum(a, x)
    far = small > 0.41421356 * big
    t = jnp.where(far, small - big, small) / jnp.where(far, small + big, big)
    z = t * t
    p = ((8.05374449538e-2 * z - 1.38776856032e-1) * z + 1.99777106478e-1) * z - 3.33329491539e-1
    r = p * z * t + t + jnp.where(far, math.pi / 4, 0.0)
    r = jnp.where(a > x, math.pi / 2 - r, r)
    return jnp.where(y < 0, -r, r)


def rim_kernel(
    yb_ref, ya_ref, xb_ref, xa_ref, rs_ref, tl_ref, tr_ref, pl_ref, pr_ref, g_ref, lr_ref, m_ref, v_ref,
    nr_ref, nm_ref, nv_ref, row_s, col_s, row_scr, col_scr, row_sh, col_sh, row_ac, col_ac, row_g, col_g, turn_scr, side_scr,
):
    gx, nx = place("gx")
    gy, _ = place("gy")
    even_x, even_y = gx % 2 == 0, gy % 2 == 0
    height, lanes = lr_ref.shape
    for f in range(NF):
        r = slice(3 * f, 3 * f + 3)
        ya, yb = ya_ref[r, :], yb_ref[r, :]
        row_s[f, 0:8, :] = jnp.ones((8, lanes), jnp.float32)
        row_s[f, 24:32, :] = jnp.ones((8, lanes), jnp.float32)
        row_s[f, 5:8, :] = jnp.where(even_y, yb, ya)
        row_s[f, 24:27, :] = jnp.where(even_y, ya, yb)
        row_s[f, 8:24, :] = rs_ref[f]
    strip_gradient(row_s, row_scr, row_sh, row_ac, row_g)
    left_in = jnp.where(even_x, xb_ref[...], xa_ref[...])
    right_in = jnp.where(even_x, xa_ref[...], xb_ref[...])
    for f, t in enumerate(TURNED):
        shift = (125 - 6 * f) % 128
        r = slice(3 * f, 3 * f + 3)
        col_s[t, 0:8, :] = jnp.ones((8, height + 128), jnp.float32)
        col_s[t, 24:32, :] = jnp.ones((8, height + 128), jnp.float32)
        col_s[t, 5:8, 0:height] = left_in[r, :]
        col_s[t, 24:27, 0:height] = right_in[r, :]
        col_s[t, 8:16, 0:height] = tl_ref[f]
        col_s[t, 16:24, 0:height] = tr_ref[f]
        col_s[t, 5:8, height:] = pltpu.roll(left_in[32:40, 0:128], shift, 1)[0:3, :]
        col_s[t, 24:27, height:] = pltpu.roll(right_in[32:40, 0:128], shift, 1)[0:3, :]
        col_s[t, 8:16, height:] = pltpu.roll(pl_ref[...], shift, 1)
        col_s[t, 16:24, height:] = pltpu.roll(pr_ref[...], shift, 1)
    strip_gradient(col_s, col_scr, col_sh, col_ac, col_g)
    turn_scr[...] = jnp.zeros_like(turn_scr)
    turn_scr[0:8, :] = col_g[8:16, 0:height]
    turn_scr[120:128, :] = col_g[16:24, 0:height]
    side_scr[...] = turn_scr[...].T
    lane = lax.broadcasted_iota(jnp.int32, (16, lanes), 1)
    beside = (lane < 3) | (lane >= lanes - 3)

    def update(r, rim):
        g = rim(g_ref[r, :])
        side = side_scr[r, :]
        g = jnp.where(beside, jnp.concatenate([side] * (lanes // 128), 1), g)
        nm = BETA_ONE * m_ref[r, :] + (1.0 - BETA_ONE) * g
        nv = BETA_TWO * v_ref[r, :] + (1.0 - BETA_TWO) * g * g
        nm_ref[r, :] = nm
        nv_ref[r, :] = nv
        root = jnp.sqrt(nv * (1.0 / (1.0 - BETA_TWO**UPDATES)))
        turn = arctan_ratio(nm * (1.0 / (1.0 - BETA_ONE**UPDATES)), root)
        nr_ref[r, :] = lr_ref[r, :] - (LEARN_RATE * ATAN_SCALE) * turn

    def inside(i, carry):
        update(pl.ds(pl.multiple_of(i * 16, 16), 16), lambda g: g)
        return carry

    row = lax.broadcasted_iota(jnp.int32, (16, lanes), 0)
    update(slice(0, 16), lambda g: jnp.where(row < 3, row_g[8:24, :], g))
    lax.fori_loop(1, height // 16 - 1, inside, 0)
    update(slice(height - 16, height), lambda g: jnp.where(row >= 13, row_g[8:24, :], g))


def swap_pairs(n, odd):
    pairs = []
    for i in range(n):
        j = i ^ 1 if not odd else ((i + 1) ^ 1) - 1
        pairs.append((i, j if 0 <= j < n else i))
    return pairs


def call(kernel, out_shapes, scratch=(), in_specs=None, flops=0, name=None, vmem_mb=VMEM_MB):
    params = pltpu.CompilerParams(vmem_limit_bytes=vmem_mb << 20)
    shapes = [jax.ShapeDtypeStruct(s, jnp.float32) for s in out_shapes]
    kwargs = {} if in_specs is None else {"in_specs": in_specs}
    return pl.pallas_call(
        kernel,
        out_shape=shapes,
        scratch_shapes=list(scratch),
        compiler_params=params,
        cost_estimate=pl.CostEstimate(flops=flops, bytes_accessed=flops // 8, transcendentals=0),
        name=name,
        **kwargs,
    )


def on_device(water, ground, rough, moment, second, wet_tiles, cot):
    height, lanes = ground.shape
    hbm = pl.BlockSpec(memory_space=pltpu.HBM)
    y_b, y_a, wet = call(
        pack_rows_kernel,
        [(32, lanes), (32, lanes), (16, lanes)],
        scratch=[
            pltpu.SMEM((2, 2), jnp.int32),
            pltpu.VMEM((8, 8, lanes), jnp.float32),
            pltpu.VMEM((8, 8, lanes), jnp.float32),
            pltpu.SemaphoreType.DMA((9,)),
        ],
        in_specs=[hbm] * 5,
        name="pack_rows",
        vmem_mb=12,
    )(*(pltpu.with_memory_space_constraint(x, pltpu.HBM) for x in (wet_tiles, water, ground, rough, cot)))
    ny, nx = lax.axis_size("gy"), lax.axis_size("gx")
    y_b = lax.ppermute(y_b, "gy", swap_pairs(ny, True))
    y_a = lax.ppermute(y_a, "gy", swap_pairs(ny, False))
    scratch = [
        pltpu.VMEM((N_SHIFTED, lanes // 128, height + 16, 128), jnp.float32),
        pltpu.VMEM((N_ACROSS, height, lanes), jnp.float32),
    ]
    ahead, row_own, col_left, col_right = call(
        forward_kernel,
        [(N_AHEAD, height, lanes), (NF, 16, lanes), (NF, 8, height), (NF, 8, height)],
        scratch=scratch,
        flops=20_000_000,
        name="forward",
    )(wet, water, ground, rough, cot)
    x_b, x_a, corner_left, corner_right = call(
        pack_cols_kernel,
        [(40, height), (40, height), (8, 128), (8, 128)],
        scratch=[pltpu.VMEM((128, 128), jnp.float32)],
        name="pack_cols",
    )(y_b, y_a, col_left, col_right)
    (grad,) = call(
        backward_kernel,
        [(height, lanes)],
        scratch=scratch,
        flops=20_000_000,
        name="backward",
    )(corner_left, wet, rough, cot, ahead)
    x_b = lax.ppermute(x_b, "gx", swap_pairs(nx, True))
    x_a = lax.ppermute(x_a, "gx", swap_pairs(nx, False))
    return tuple(
        call(
            rim_kernel,
            [(height, lanes)] * 3,
            scratch=[
                pltpu.VMEM((NF, 32, lanes), jnp.float32),
                pltpu.VMEM((NF, 32, height + 128), jnp.float32),
                pltpu.VMEM((N_AHEAD, 32, lanes), jnp.float32),
                pltpu.VMEM((N_AHEAD, 32, height + 128), jnp.float32),
                pltpu.VMEM((N_SHIFTED, lanes // 128, 48, 128), jnp.float32),
                pltpu.VMEM((N_SHIFTED, height // 128 + 1, 48, 128), jnp.float32),
                pltpu.VMEM((N_ACROSS, 32, lanes), jnp.float32),
                pltpu.VMEM((N_ACROSS, 32, height + 128), jnp.float32),
                pltpu.VMEM((32, lanes), jnp.float32),
                pltpu.VMEM((32, height + 128), jnp.float32),
                pltpu.VMEM((128, height), jnp.float32),
                pltpu.VMEM((height, 128), jnp.float32),
            ],
            name="rim",
        )(
            y_b, y_a, x_b, x_a, row_own, col_left, col_right, corner_left, corner_right,
            grad, rough, moment, second,
        )
    )


def solution(mesh):
    flat = P("gy", "gx")
    deep = P(None, "gy", "gx")
    return jax.shard_map(
        on_device,
        mesh=mesh,
        in_specs=(deep, flat, flat, flat, flat, flat, deep),
        out_specs=(flat, flat, flat),
        check_vma=False,
    )
```

```python
import math

import jax
import jax.numpy as jnp
from jax import lax
from jax.experimental import pallas as pl
from jax.experimental.pallas import tpu as pltpu
from jax.sharding import PartitionSpec as P

UPDATES = 20
GRAVITY = 9.81
HALF_STEP = 0.05
LOG_DRAG = math.log(9.81)
SPEED_EPS = 0.0001
BETA_ONE = 0.9
BETA_TWO = 0.999
LEARN_RATE = 0.05
ATAN_SCALE = 1.27
H, QX, QY, Z, LR, CH, CX, CY, WET = range(9)
NF = 9
TURNED = (H, QY, QX, Z, LR, CH, CY, CX, WET)
BLK = 8
UNROLL = 8
VMEM_MB = 12


def from_prev_col(x):
    return pltpu.roll(x, 1, 1)


def from_next_col(x):
    return pltpu.roll(x, x.shape[1] - 1, 1)


def flux_parts(h, qx, qy, slope_x, slope_y):
    inv = 1.0 / h
    u, v = qx * inv, qy * inv
    press = (0.5 * GRAVITY) * h * h
    k = HALF_STEP
    fx1, fy1 = k * qx, k * qy
    fx2, fxy, fy3 = k * (qx * u + press), k * (qx * v), k * (qy * v + press)
    h4, x4, y4 = 0.25 * h, 0.25 * qx, 0.25 * qy
    cols = [
        from_prev_col(h4 + fx1) + from_next_col(h4 - fx1),
        from_prev_col(x4 + fx2) + from_next_col(x4 - fx2) - h * slope_x,
        from_prev_col(y4 + fxy) + from_next_col(y4 - fxy) - h * slope_y,
    ]
    down = [h4 + fy1, x4 + fxy, y4 + fy3]
    up = [h4 - fy1, x4 - fxy, y4 - fy3]
    return cols, down, up, u, v


def drag_parts(h, qx, qy, rough):
    s2 = qx * qx + qy * qy + SPEED_EPS
    rs = lax.rsqrt(s2)
    b = jnp.exp(2.0 * rough + LOG_DRAG - (7.0 / 3.0) * jnp.log(h)) * (s2 * rs)
    w = 1.0 / (1.0 + b)
    return b, w, rs * rs


def rows(j):
    if isinstance(j, int):
        return slice(j * BLK, j * BLK + BLK)
    return pl.ds(pl.multiple_of(j * BLK, BLK), BLK)


def take(ref, j, off=0):
    r = pl.ds(j * BLK + 8 + off, BLK)
    if off == 0 and not isinstance(j, int):
        r = pl.ds(pl.multiple_of(j * BLK + 8, 8), BLK)
    return jnp.concatenate([ref[t, r, :] for t in range(ref.shape[0])], 1)


def give(ref, j, value):
    put(ref, pl.ds(pl.multiple_of(j * BLK + 8, 8), BLK), value)


def put(ref, r, value, at=0):
    for t in range(value.shape[1] // 128):
        ref[at + t, r, :] = value[:, 128 * t : 128 * t + 128]


def looped(n, step):
    if n <= 8:
        for j in range(n):
            step(j)
        return

    def body(j, carry):
        step(j)
        return carry

    lax.fori_loop(0, n, body, 0, unroll=UNROLL)


UH, UX, UY, SX, SY, GA, GB = range(7)
N_AHEAD, N_ACROSS, N_SHIFTED = 7, 6, 9
DOWN, UP, ZS = 0, 3, 6
PH, PX, PY = range(3)
ADJ = 6
VU, VV, PG = 3, 4, 5


def gathered(shifted, across, j):
    r = rows(j)
    return [
        take(shifted.at[DOWN + f], j, -1) + take(shifted.at[UP + f], j, 1) + across[f, r, :]
        for f in range(3)
    ]


def first_pass(get, wet, n, scr, shifted, across):
    looped(n, lambda j: give(shifted.at[ZS], j, get(Z, j)))

    def parts(j):
        r = rows(j)
        kg = HALF_STEP * GRAVITY
        z = get(Z, j)
        sx = kg * (from_next_col(z) - from_prev_col(z))
        sy = kg * (take(shifted.at[ZS], j, 1) - take(shifted.at[ZS], j, -1))
        scr[SX, r, :] = sx
        scr[SY, r, :] = sy
        cols, down, up, _, _ = flux_parts(get(H, j), get(QX, j), get(QY, j), sx, sy)
        for f in range(3):
            across[f, r, :] = cols[f]
            give(shifted.at[DOWN + f], j, down[f])
            give(shifted.at[UP + f], j, up[f])

    looped(n, parts)

    def finish(j):
        r = rows(j)
        h, qx, qy = gathered(shifted, across, j)
        b, w, _ = drag_parts(h, qx, qy, get(LR, j))
        m = wet(j)
        scr[UH, r, :] = jnp.where(m, h, get(H, j))
        scr[UX, r, :] = jnp.where(m, qx * w, get(QX, j))
        scr[UY, r, :] = jnp.where(m, qy * w, get(QY, j))
        t = jnp.where(m, -2.0 * b * w * w, 0.0)
        scr[GA, r, :] = t * qx
        scr[GB, r, :] = t * qy

    looped(n, finish)


def last_passes(get, wet, n, scr, shifted, across, put_grad):
    def parts(j):
        r = rows(j)
        cols, down, up, u, v = flux_parts(*(scr[f, r, :] for f in (UH, UX, UY, SX, SY)))
        across[VU, r, :] = u
        across[VV, r, :] = v
        for f in range(3):
            across[f, r, :] = cols[f]
            give(shifted.at[DOWN + f], j, down[f])
            give(shifted.at[UP + f], j, up[f])

    looped(n, parts)

    def finish(j):
        h, qx, qy = gathered(shifted, across, j)
        b, w, inv_s2 = drag_parts(h, qx, qy, get(LR, j))
        m = wet(j)
        ch, cx, cy = get(CH, j), get(CX, j), get(CY, j)
        t = (cx * qx + cy * qy) * (w * w) * b
        ts = t * inv_s2
        return [
            jnp.where(m, ch + (7.0 / 3.0) * t / h, 0.0),
            jnp.where(m, cx * w - ts * qx, 0.0),
            jnp.where(m, cy * w - ts * qy, 0.0),
            jnp.where(m, -2.0 * t, 0.0),
        ]

    def finish_all(j):
        for f, value in enumerate(finish(j)):
            if f < 3:
                give(shifted.at[ADJ + f], j, value)
            else:
                across[PG, rows(j), :] = value

    looped(n, finish_all)

    def back(j):
        r = rows(j)

        def four(f):
            ref = shifted.at[ADJ + f]
            cur = take(ref, j)
            return from_next_col(cur), from_prev_col(cur), take(ref, j, 1), take(ref, j, -1)

        he, hw, hs, hn = four(PH)
        xe, xw, xs, xn = four(PX)
        ye, yw, ys, yn = four(PY)
        u, v = across[VU, r, :], across[VV, r, :]
        k = HALF_STEP
        cross = k * ((ye - yw) + (xs - xn))
        cot_x = (
            0.25 * ((xe + xw) + (xs + xn))
            + k * (he - hw)
            + (2.0 * k) * u * (xe - xw)
            + v * cross
        )
        cot_y = (
            0.25 * ((ye + yw) + (ys + yn))
            + k * (hs - hn)
            + (2.0 * k) * v * (ys - yn)
            + u * cross
        )
        put_grad(j, across[PG, r, :] + scr[GA, r, :] * cot_x + scr[GB, r, :] * cot_y)

    looped(n, back)


def place(axis):
    index = lax.axis_index(axis)
    return index, lax.axis_size(axis)


def three_rows(block, first, mirrored, sign):
    natural = block[first : first + 3, :]
    reverse = jnp.concatenate([block[first + 2 - d : first + 3 - d, :] for d in range(3)], 0)
    return jnp.where(mirrored, sign * reverse, natural)


def pack_rows_kernel(wet_hbm, w_hbm, z_hbm, lr_hbm, c_hbm, b_ref, a_ref, wet_ref, wet_s, top, bot, sems):
    height, lanes = z_hbm.shape
    copies = [pltpu.make_async_copy(wet_hbm, wet_s, sems.at[0])]
    for side, (buf, row) in enumerate(((top, 0), (bot, height - 8))):
        r = pl.ds(row, 8)
        for at, (src, dst) in enumerate((
            (w_hbm.at[:, r, :], buf.at[pl.ds(0, 3)]),
            (z_hbm.at[r, :], buf.at[Z]),
            (lr_hbm.at[r, :], buf.at[LR]),
            (c_hbm.at[:, r, :], buf.at[pl.ds(CH, 3)]),
        )):
            copies.append(pltpu.make_async_copy(src, dst, sems.at[1 + 4 * side + at]))
    for copy in copies:
        copy.start()
    gy, ny = place("gy")
    even = gy % 2 == 0
    lane = lax.broadcasted_iota(jnp.int32, (8, lanes), 1)
    a_ref[24:32, :] = jnp.zeros((8, lanes), jnp.float32)
    b_ref[24:32, :] = jnp.zeros((8, lanes), jnp.float32)
    for copy in copies:
        copy.wait()
    for row in range(2):
        left = (wet_s[row, 0] > 0).astype(jnp.float32)
        right = (wet_s[row, 1] > 0).astype(jnp.float32)
        wet_ref[8 * row : 8 * row + 8, :] = jnp.where(lane < lanes // 2, left, right)
    for f in range(NF):
        sign = -1.0 if f in (QY, CY) else 1.0
        t = three_rows(top[f] if f < WET else wet_ref[0:8, :], 0, gy == 0, sign)
        b = three_rows(bot[f] if f < WET else wet_ref[8:16, :], 5, gy == ny - 1, sign)
        a_ref[3 * f : 3 * f + 3, :] = jnp.where(even, b, t)
        b_ref[3 * f : 3 * f + 3, :] = jnp.where(even, t, b)


def tile_wet(wet_ref, j, n):
    return wet_ref[rows(j // (n // 2)), :] > 0.5


def forward_kernel(wet_ref, w_ref, z_ref, lr_ref, c_ref, scr, rs_ref, tl_ref, tr_ref, shifted, across):
    height, lanes = z_ref.shape
    n = height // BLK

    def field(f):
        if f <= QY:
            return w_ref.at[f]
        return z_ref if f == Z else lr_ref if f == LR else c_ref.at[f - CH]

    def get(f, j):
        return field(f)[rows(j), :]

    first_pass(get, lambda j: tile_wet(wet_ref, j, n), n, scr, shifted, across)
    lane = lax.broadcasted_iota(jnp.int32, (height, 128), 1)
    for f in range(WET):
        ref = field(f)
        rs_ref[f, 0:8, :] = ref[0:8, :]
        rs_ref[f, 8:16, :] = ref[height - 8 : height, :]
        turned = jnp.where(lane < 64, ref[:, 0:128], ref[:, lanes - 128 : lanes]).T
        tl_ref[f] = turned[0:8, :]
        tr_ref[f] = turned[120:128, :]
    top, bottom = wet_ref[0:8, :], wet_ref[8:16, :]
    rs_ref[WET, 0:8, :] = top
    rs_ref[WET, 8:16, :] = bottom
    half = lanes // 2
    tl_ref[WET] = jnp.concatenate([top[:, :half], bottom[:, :half]], 1)
    tr_ref[WET] = jnp.concatenate([top[:, half:], bottom[:, half:]], 1)


def backward_kernel(after_ref, wet_ref, lr_ref, c_ref, scr, g_ref, shifted, across):
    n = lr_ref.shape[0] // BLK

    def get(f, j):
        return (lr_ref if f == LR else c_ref.at[f - CH])[rows(j), :]

    def put_grad(j, value):
        g_ref[rows(j), :] = value

    last_passes(get, lambda j: tile_wet(wet_ref, j, n), n, scr, shifted, across, put_grad)


def pack_cols_kernel(yb_ref, ya_ref, yw_ref, tl_ref, tr_ref, b_ref, a_ref, pl_ref, pr_ref, k_scr):
    gx, nx = place("gx")
    gy, ny = place("gy")
    even_y = gy % 2 == 0
    lanes = ya_ref.shape[1]
    y_b = jnp.where((gy == 0) | (gy == ny - 1), yw_ref[...], yb_ref[...])
    below = jnp.where(even_y, ya_ref[...], y_b)
    above = jnp.where(even_y, y_b, ya_ref[...])
    lane = lax.broadcasted_iota(jnp.int32, (above.shape[0], 128), 1)
    above = jnp.where(lane < 64, above[:, 0:128], above[:, lanes - 128 : lanes])
    below = jnp.where(lane < 64, below[:, 0:128], below[:, lanes - 128 : lanes])
    k_scr[...] = jnp.zeros_like(k_scr)
    for f in range(NF):
        k_scr[6 * f : 6 * f + 3, :] = above[3 * f : 3 * f + 3, :]
        k_scr[6 * f + 3 : 6 * f + 6, :] = below[3 * f : 3 * f + 3, :]
    turned = k_scr[...].T
    left_corner, right_corner = turned[0:8, :], turned[120:128, :]
    pl_ref[...] = left_corner
    pr_ref[...] = right_corner
    even = gx % 2 == 0
    a_ref[...] = jnp.zeros_like(a_ref)
    b_ref[...] = jnp.zeros_like(b_ref)
    first, last = gx == 0, gx == nx - 1
    for f in range(NF):
        sign = -1.0 if f in (QX, CX) else 1.0
        t = three_rows(tl_ref[f], 0, first, sign)
        b = three_rows(tr_ref[f], 5, last, sign)
        a_ref[3 * f : 3 * f + 3, :] = jnp.where(even, b, t)
        b_ref[3 * f : 3 * f + 3, :] = jnp.where(even, t, b)
    lane = lax.broadcasted_iota(jnp.int32, (3, 128), 1)
    flip = ((lane >= 6 * QX) & (lane < 6 * QX + 6)) | ((lane >= 6 * CX) & (lane < 6 * CX + 6))
    sign = jnp.where(flip, -1.0, 1.0)
    t = three_rows(left_corner, 0, first, sign)
    b = three_rows(right_corner, 5, last, sign)
    a_ref[32:35, 0:128] = jnp.where(even, b, t)
    b_ref[32:35, 0:128] = jnp.where(even, t, b)


def strip_gradient(s_ref, scr, shifted, across, g_ref):
    n = s_ref.shape[1] // BLK

    def get(f, j):
        return s_ref[f, rows(j), :]

    def wet(j):
        return get(WET, j) > 0.5

    def put_grad(j, value):
        g_ref[rows(j), :] = value

    first_pass(get, wet, n, scr, shifted, across)
    last_passes(get, wet, n, scr, shifted, across, put_grad)


def arctan_ratio(y, x):
    a = jnp.abs(y)
    big, small = jnp.maximum(a, x), jnp.minimum(a, x)
    far = small > 0.41421356 * big
    t = jnp.where(far, small - big, small) / jnp.where(far, small + big, big)
    z = t * t
    p = ((8.05374449538e-2 * z - 1.38776856032e-1) * z + 1.99777106478e-1) * z - 3.33329491539e-1
    r = p * z * t + t + jnp.where(far, math.pi / 4, 0.0)
    r = jnp.where(a > x, math.pi / 2 - r, r)
    return jnp.where(y < 0, -r, r)


def rim_kernel(
    yb_ref, ya_ref, yw_ref, xb_ref, xa_ref, xw_ref, rs_ref, tl_ref, tr_ref, pl_ref, pr_ref, g_ref, lr_ref, m_ref, v_ref,
    nr_ref, nm_ref, nv_ref, row_s, col_s, row_scr, col_scr, row_sh, col_sh, row_ac, col_ac, row_g, col_g, turn_scr, side_scr,
):
    gx, nx = place("gx")
    gy, ny = place("gy")
    even_x, even_y = gx % 2 == 0, gy % 2 == 0
    at_wall_x, at_wall_y = (gx == 0) | (gx == nx - 1), (gy == 0) | (gy == ny - 1)
    height, lanes = lr_ref.shape
    for f in range(NF):
        r = slice(3 * f, 3 * f + 3)
        ya, yb = ya_ref[r, :], jnp.where(at_wall_y, yw_ref[r, :], yb_ref[r, :])
        row_s[f, 0:8, :] = jnp.ones((8, lanes), jnp.float32)
        row_s[f, 24:32, :] = jnp.ones((8, lanes), jnp.float32)
        row_s[f, 5:8, :] = jnp.where(even_y, yb, ya)
        row_s[f, 24:27, :] = jnp.where(even_y, ya, yb)
        row_s[f, 8:24, :] = rs_ref[f]
    strip_gradient(row_s, row_scr, row_sh, row_ac, row_g)
    x_b = jnp.where(at_wall_x, xw_ref[...], xb_ref[...])
    left_in = jnp.where(even_x, x_b, xa_ref[...])
    right_in = jnp.where(even_x, xa_ref[...], x_b)
    for f, t in enumerate(TURNED):
        shift = (125 - 6 * f) % 128
        r = slice(3 * f, 3 * f + 3)
        col_s[t, 0:8, :] = jnp.ones((8, height + 128), jnp.float32)
        col_s[t, 24:32, :] = jnp.ones((8, height + 128), jnp.float32)
        col_s[t, 5:8, 0:height] = left_in[r, :]
        col_s[t, 24:27, 0:height] = right_in[r, :]
        col_s[t, 8:16, 0:height] = tl_ref[f]
        col_s[t, 16:24, 0:height] = tr_ref[f]
        col_s[t, 5:8, height:] = pltpu.roll(left_in[32:40, 0:128], shift, 1)[0:3, :]
        col_s[t, 24:27, height:] = pltpu.roll(right_in[32:40, 0:128], shift, 1)[0:3, :]
        col_s[t, 8:16, height:] = pltpu.roll(pl_ref[...], shift, 1)
        col_s[t, 16:24, height:] = pltpu.roll(pr_ref[...], shift, 1)
    strip_gradient(col_s, col_scr, col_sh, col_ac, col_g)
    turn_scr[...] = jnp.zeros_like(turn_scr)
    turn_scr[0:8, :] = col_g[8:16, 0:height]
    turn_scr[120:128, :] = col_g[16:24, 0:height]
    side_scr[...] = turn_scr[...].T
    lane = lax.broadcasted_iota(jnp.int32, (16, lanes), 1)
    beside = (lane < 3) | (lane >= lanes - 3)

    def update(r, rim):
        g = rim(g_ref[r, :])
        side = side_scr[r, :]
        g = jnp.where(beside, jnp.concatenate([side] * (lanes // 128), 1), g)
        nm = BETA_ONE * m_ref[r, :] + (1.0 - BETA_ONE) * g
        nv = BETA_TWO * v_ref[r, :] + (1.0 - BETA_TWO) * g * g
        nm_ref[r, :] = nm
        nv_ref[r, :] = nv
        root = jnp.sqrt(nv * (1.0 / (1.0 - BETA_TWO**UPDATES)))
        turn = arctan_ratio(nm * (1.0 / (1.0 - BETA_ONE**UPDATES)), root)
        nr_ref[r, :] = lr_ref[r, :] - (LEARN_RATE * ATAN_SCALE) * turn

    def inside(i, carry):
        update(pl.ds(pl.multiple_of(i * 16, 16), 16), lambda g: g)
        return carry

    row = lax.broadcasted_iota(jnp.int32, (16, lanes), 0)
    update(slice(0, 16), lambda g: jnp.where(row < 3, row_g[8:24, :], g))
    lax.fori_loop(1, height // 16 - 1, inside, 0)
    update(slice(height - 16, height), lambda g: jnp.where(row >= 13, row_g[8:24, :], g))


def swap_pairs(nx, ny, axis, odd):
    pairs = []
    for x in range(nx):
        for y in range(ny):
            u, v = x, y
            if axis == "gx":
                u = x ^ 1 if not odd else ((x + 1) ^ 1) - 1
                if not 0 <= u < nx:
                    u, v = x, y ^ 1
            else:
                v = y ^ 1 if not odd else ((y + 1) ^ 1) - 1
                if not 0 <= v < ny:
                    u, v = x ^ 1, y
            pairs.append((x * ny + y, u * ny + v))
    return pairs


def swapped(value, axis, odd):
    pairs = swap_pairs(lax.axis_size("gx"), lax.axis_size("gy"), axis, odd)
    return lax.ppermute(value, ("gx", "gy"), pairs)


def call(kernel, out_shapes, scratch=(), in_specs=None, flops=0, vmem_mb=VMEM_MB):
    params = pltpu.CompilerParams(vmem_limit_bytes=vmem_mb << 20)
    shapes = [jax.ShapeDtypeStruct(s, jnp.float32) for s in out_shapes]
    kwargs = {} if in_specs is None else {"in_specs": in_specs}
    return pl.pallas_call(
        kernel,
        out_shape=shapes,
        scratch_shapes=list(scratch),
        compiler_params=params,
        cost_estimate=pl.CostEstimate(flops=flops, bytes_accessed=flops // 8, transcendentals=0),
        **kwargs,
    )


def on_device(water, ground, rough, moment, second, wet_tiles, cot):
    height, lanes = ground.shape
    hbm = pl.BlockSpec(memory_space=pltpu.HBM)
    y_b, y_a, wet = call(
        pack_rows_kernel,
        [(32, lanes), (32, lanes), (16, lanes)],
        scratch=[
            pltpu.SMEM((2, 2), jnp.int32),
            pltpu.VMEM((8, 8, lanes), jnp.float32),
            pltpu.VMEM((8, 8, lanes), jnp.float32),
            pltpu.SemaphoreType.DMA((9,)),
        ],
        in_specs=[hbm] * 5,
        vmem_mb=12,
    )(*(pltpu.with_memory_space_constraint(x, pltpu.HBM) for x in (wet_tiles, water, ground, rough, cot)))
    y_wall, y_b, y_a = y_b, swapped(y_b, "gy", True), swapped(y_a, "gy", False)
    scratch = [
        pltpu.VMEM((N_SHIFTED, lanes // 128, height + 16, 128), jnp.float32),
        pltpu.VMEM((N_ACROSS, height, lanes), jnp.float32),
    ]
    ahead, row_own, col_left, col_right = call(
        forward_kernel,
        [(N_AHEAD, height, lanes), (NF, 16, lanes), (NF, 8, height), (NF, 8, height)],
        scratch=scratch,
        flops=20_000_000,
    )(wet, water, ground, rough, cot)
    x_b, x_a, corner_left, corner_right = call(
        pack_cols_kernel,
        [(40, height), (40, height), (8, 128), (8, 128)],
        scratch=[pltpu.VMEM((128, 128), jnp.float32)],
    )(y_b, y_a, y_wall, col_left, col_right)
    (grad,) = call(
        backward_kernel, [(height, lanes)], scratch=scratch, flops=20_000_000
    )(corner_left, wet, rough, cot, ahead)
    x_wall, x_b, x_a = x_b, swapped(x_b, "gx", True), swapped(x_a, "gx", False)
    return tuple(
        call(
            rim_kernel,
            [(height, lanes)] * 3,
            scratch=[
                pltpu.VMEM((NF, 32, lanes), jnp.float32),
                pltpu.VMEM((NF, 32, height + 128), jnp.float32),
                pltpu.VMEM((N_AHEAD, 32, lanes), jnp.float32),
                pltpu.VMEM((N_AHEAD, 32, height + 128), jnp.float32),
                pltpu.VMEM((N_SHIFTED, lanes // 128, 48, 128), jnp.float32),
                pltpu.VMEM((N_SHIFTED, height // 128 + 1, 48, 128), jnp.float32),
                pltpu.VMEM((N_ACROSS, 32, lanes), jnp.float32),
                pltpu.VMEM((N_ACROSS, 32, height + 128), jnp.float32),
                pltpu.VMEM((32, lanes), jnp.float32),
                pltpu.VMEM((32, height + 128), jnp.float32),
                pltpu.VMEM((128, height), jnp.float32),
                pltpu.VMEM((height, 128), jnp.float32),
            ],
        )(
            y_b, y_a, y_wall, x_b, x_a, x_wall, row_own, col_left, col_right, corner_left, corner_right,
            grad, rough, moment, second,
        )
    )


def solution(mesh):
    flat = P("gy", "gx")
    deep = P(None, "gy", "gx")

    return jax.shard_map(
        on_device,
        mesh=mesh,
        in_specs=(deep, flat, flat, flat, flat, flat, deep),
        out_specs=(flat, flat, flat),
        check_vma=False,
    )
```

```python
import math

import jax
import jax.numpy as jnp
from jax import lax
from jax.experimental import pallas as pl
from jax.experimental.pallas import tpu as pltpu
from jax.sharding import PartitionSpec as P

UPDATES = 20
GRAVITY = 9.81
HALF_STEP = 0.05
LOG_DRAG = math.log(9.81)
SPEED_EPS = 0.0001
BETA_ONE = 0.9
BETA_TWO = 0.999
LEARN_RATE = 0.05
ATAN_SCALE = 1.27
H, QX, QY, Z, LR, CH, CX, CY, WET = range(9)
NF = 9
TURNED = (H, QY, QX, Z, LR, CH, CY, CX, WET)
BLK = 8
UNROLL = 8
VMEM_MB = 12


def from_prev_col(x):
    return pltpu.roll(x, 1, 1)


def from_next_col(x):
    return pltpu.roll(x, x.shape[1] - 1, 1)


def flux_parts(h, qx, qy, slope_x, slope_y):
    inv = 1.0 / h
    u, v = qx * inv, qy * inv
    press = (0.5 * GRAVITY) * h * h
    k = HALF_STEP
    fx1, fy1 = k * qx, k * qy
    fx2, fxy, fy3 = k * (qx * u + press), k * (qx * v), k * (qy * v + press)
    h4, x4, y4 = 0.25 * h, 0.25 * qx, 0.25 * qy
    cols = [
        from_prev_col(h4 + fx1) + from_next_col(h4 - fx1),
        from_prev_col(x4 + fx2) + from_next_col(x4 - fx2) - h * slope_x,
        from_prev_col(y4 + fxy) + from_next_col(y4 - fxy) - h * slope_y,
    ]
    down = [h4 + fy1, x4 + fxy, y4 + fy3]
    up = [h4 - fy1, x4 - fxy, y4 - fy3]
    return cols, down, up, u, v


def drag_parts(h, qx, qy, rough):
    s2 = qx * qx + qy * qy + SPEED_EPS
    rs = lax.rsqrt(s2)
    b = jnp.exp(2.0 * rough + LOG_DRAG - (7.0 / 3.0) * jnp.log(h)) * (s2 * rs)
    w = 1.0 / (1.0 + b)
    return b, w, rs * rs


def rows(j):
    if isinstance(j, int):
        return slice(j * BLK, j * BLK + BLK)
    return pl.ds(pl.multiple_of(j * BLK, BLK), BLK)


def take(ref, j, off=0):
    r = pl.ds(j * BLK + 8 + off, BLK)
    if off == 0 and not isinstance(j, int):
        r = pl.ds(pl.multiple_of(j * BLK + 8, 8), BLK)
    return jnp.concatenate([ref[t, r, :] for t in range(ref.shape[0])], 1)


def give(ref, j, value):
    put(ref, pl.ds(pl.multiple_of(j * BLK + 8, 8), BLK), value)


def put(ref, r, value, at=0):
    for t in range(value.shape[1] // 128):
        ref[at + t, r, :] = value[:, 128 * t : 128 * t + 128]


def looped(n, step):
    if n <= 8:
        for j in range(n):
            step(j)
        return

    def body(j, carry):
        step(j)
        return carry

    lax.fori_loop(0, n, body, 0, unroll=UNROLL)


UH, UX, UY, SX, SY, GA, GB = range(7)
N_AHEAD, N_ACROSS, N_SHIFTED = 7, 6, 9
DOWN, UP, ZS = 0, 3, 6
PH, PX, PY = range(3)
ADJ = 6
VU, VV, PG = 3, 4, 5


def gathered(shifted, across, j):
    r = rows(j)
    return [
        take(shifted.at[DOWN + f], j, -1) + take(shifted.at[UP + f], j, 1) + across[f, r, :]
        for f in range(3)
    ]


def first_pass(get, wet, n, scr, shifted, across):
    looped(n, lambda j: give(shifted.at[ZS], j, get(Z, j)))

    def parts(j):
        r = rows(j)
        kg = HALF_STEP * GRAVITY
        z = get(Z, j)
        sx = kg * (from_next_col(z) - from_prev_col(z))
        sy = kg * (take(shifted.at[ZS], j, 1) - take(shifted.at[ZS], j, -1))
        scr[SX, r, :] = sx
        scr[SY, r, :] = sy
        cols, down, up, _, _ = flux_parts(get(H, j), get(QX, j), get(QY, j), sx, sy)
        for f in range(3):
            across[f, r, :] = cols[f]
            give(shifted.at[DOWN + f], j, down[f])
            give(shifted.at[UP + f], j, up[f])

    looped(n, parts)

    def finish(j):
        r = rows(j)
        h, qx, qy = gathered(shifted, across, j)
        b, w, _ = drag_parts(h, qx, qy, get(LR, j))
        m = wet(j)
        scr[UH, r, :] = jnp.where(m, h, get(H, j))
        scr[UX, r, :] = jnp.where(m, qx * w, get(QX, j))
        scr[UY, r, :] = jnp.where(m, qy * w, get(QY, j))
        t = jnp.where(m, -2.0 * b * w * w, 0.0)
        scr[GA, r, :] = t * qx
        scr[GB, r, :] = t * qy

    looped(n, finish)


def second_pass(get, wet, n, scr, shifted, across):
    def parts(j):
        r = rows(j)
        cols, down, up, u, v = flux_parts(*(scr[f, r, :] for f in (UH, UX, UY, SX, SY)))
        across[VU, r, :] = u
        across[VV, r, :] = v
        for f in range(3):
            across[f, r, :] = cols[f]
            give(shifted.at[DOWN + f], j, down[f])
            give(shifted.at[UP + f], j, up[f])

    looped(n, parts)

    def finish(j):
        h, qx, qy = gathered(shifted, across, j)
        b, w, inv_s2 = drag_parts(h, qx, qy, get(LR, j))
        m = wet(j)
        ch, cx, cy = get(CH, j), get(CX, j), get(CY, j)
        t = (cx * qx + cy * qy) * (w * w) * b
        ts = t * inv_s2
        return [
            jnp.where(m, ch + (7.0 / 3.0) * t / h, 0.0),
            jnp.where(m, cx * w - ts * qx, 0.0),
            jnp.where(m, cy * w - ts * qy, 0.0),
            jnp.where(m, -2.0 * t, 0.0),
        ]

    def finish_all(j):
        for f, value in enumerate(finish(j)):
            if f < 3:
                give(shifted.at[ADJ + f], j, value)
            else:
                across[PG, rows(j), :] = value

    looped(n, finish_all)


def third_pass(n, scr, shifted, across, put_grad):
    def back(j):
        r = rows(j)

        def four(f):
            ref = shifted.at[ADJ + f]
            cur = take(ref, j)
            return from_next_col(cur), from_prev_col(cur), take(ref, j, 1), take(ref, j, -1)

        he, hw, hs, hn = four(PH)
        xe, xw, xs, xn = four(PX)
        ye, yw, ys, yn = four(PY)
        u, v = across[VU, r, :], across[VV, r, :]
        k = HALF_STEP
        cross = k * ((ye - yw) + (xs - xn))
        cot_x = (
            0.25 * ((xe + xw) + (xs + xn))
            + k * (he - hw)
            + (2.0 * k) * u * (xe - xw)
            + v * cross
        )
        cot_y = (
            0.25 * ((ye + yw) + (ys + yn))
            + k * (hs - hn)
            + (2.0 * k) * v * (ys - yn)
            + u * cross
        )
        put_grad(j, across[PG, r, :] + scr[GA, r, :] * cot_x + scr[GB, r, :] * cot_y)

    looped(n, back)


def place(axis):
    index = lax.axis_index(axis)
    return index, lax.axis_size(axis)


def three_rows(block, first, mirrored, sign):
    natural = block[first : first + 3, :]
    reverse = jnp.concatenate([block[first + 2 - d : first + 3 - d, :] for d in range(3)], 0)
    return jnp.where(mirrored, sign * reverse, natural)


def pack_rows_kernel(wet_hbm, w_hbm, z_hbm, lr_hbm, c_hbm, b_ref, a_ref, wet_ref, wet_s, top, bot, sems):
    height, lanes = z_hbm.shape
    copies = [pltpu.make_async_copy(wet_hbm, wet_s, sems.at[0])]
    for side, (buf, row) in enumerate(((top, 0), (bot, height - 8))):
        r = pl.ds(row, 8)
        for at, (src, dst) in enumerate((
            (w_hbm.at[:, r, :], buf.at[pl.ds(0, 3)]),
            (z_hbm.at[r, :], buf.at[Z]),
            (lr_hbm.at[r, :], buf.at[LR]),
            (c_hbm.at[:, r, :], buf.at[pl.ds(CH, 3)]),
        )):
            copies.append(pltpu.make_async_copy(src, dst, sems.at[1 + 4 * side + at]))
    for copy in copies:
        copy.start()
    gy, ny = place("gy")
    even = gy % 2 == 0
    lane = lax.broadcasted_iota(jnp.int32, (8, lanes), 1)
    a_ref[24:32, :] = jnp.zeros((8, lanes), jnp.float32)
    b_ref[24:32, :] = jnp.zeros((8, lanes), jnp.float32)
    for copy in copies:
        copy.wait()
    for row in range(2):
        left = (wet_s[row, 0] > 0).astype(jnp.float32)
        right = (wet_s[row, 1] > 0).astype(jnp.float32)
        wet_ref[8 * row : 8 * row + 8, :] = jnp.where(lane < lanes // 2, left, right)
    for f in range(NF):
        sign = -1.0 if f in (QY, CY) else 1.0
        t = three_rows(top[f] if f < WET else wet_ref[0:8, :], 0, gy == 0, sign)
        b = three_rows(bot[f] if f < WET else wet_ref[8:16, :], 5, gy == ny - 1, sign)
        a_ref[3 * f : 3 * f + 3, :] = jnp.where(even, b, t)
        b_ref[3 * f : 3 * f + 3, :] = jnp.where(even, t, b)


def tile_wet(wet_ref, j, n):
    return wet_ref[rows(j // (n // 2)), :] > 0.5


def forward_kernel(wet_ref, w_ref, z_ref, lr_ref, c_ref, scr, shifted, across, rs_ref, tl_ref, tr_ref):
    height, lanes = z_ref.shape
    n = height // BLK

    def field(f):
        if f <= QY:
            return w_ref.at[f]
        return z_ref if f == Z else lr_ref if f == LR else c_ref.at[f - CH]

    def get(f, j):
        return field(f)[rows(j), :]

    first_pass(get, lambda j: tile_wet(wet_ref, j, n), n, scr, shifted, across)
    second_pass(get, lambda j: tile_wet(wet_ref, j, n), n, scr, shifted, across)
    lane = lax.broadcasted_iota(jnp.int32, (height, 128), 1)
    for f in range(WET):
        ref = field(f)
        rs_ref[f, 0:8, :] = ref[0:8, :]
        rs_ref[f, 8:16, :] = ref[height - 8 : height, :]
        turned = jnp.where(lane < 64, ref[:, 0:128], ref[:, lanes - 128 : lanes]).T
        tl_ref[f] = turned[0:8, :]
        tr_ref[f] = turned[120:128, :]
    top, bottom = wet_ref[0:8, :], wet_ref[8:16, :]
    rs_ref[WET, 0:8, :] = top
    rs_ref[WET, 8:16, :] = bottom
    half = lanes // 2
    tl_ref[WET] = jnp.concatenate([top[:, :half], bottom[:, :half]], 1)
    tr_ref[WET] = jnp.concatenate([top[:, half:], bottom[:, half:]], 1)


def strip_gradient(s_ref, scr, shifted, across, g_ref):
    n = s_ref.shape[1] // BLK

    def get(f, j):
        return s_ref[f, rows(j), :]

    def wet(j):
        return get(WET, j) > 0.5

    def put_grad(j, value):
        g_ref[rows(j), :] = value

    first_pass(get, wet, n, scr, shifted, across)
    second_pass(get, wet, n, scr, shifted, across)
    third_pass(n, scr, shifted, across, put_grad)


def arctan_ratio(y, x):
    a = jnp.abs(y)
    big, small = jnp.maximum(a, x), jnp.minimum(a, x)
    far = small > 0.41421356 * big
    t = jnp.where(far, small - big, small) / jnp.where(far, small + big, big)
    z = t * t
    p = ((8.05374449538e-2 * z - 1.38776856032e-1) * z + 1.99777106478e-1) * z - 3.33329491539e-1
    r = p * z * t + t + jnp.where(far, math.pi / 4, 0.0)
    r = jnp.where(a > x, math.pi / 2 - r, r)
    return jnp.where(y < 0, -r, r)


def updated(g, rough, moment, second):
    nm = BETA_ONE * moment + (1.0 - BETA_ONE) * g
    nv = BETA_TWO * second + (1.0 - BETA_TWO) * g * g
    root = jnp.sqrt(nv * (1.0 / (1.0 - BETA_TWO**UPDATES)))
    turn = arctan_ratio(nm * (1.0 / (1.0 - BETA_ONE**UPDATES)), root)
    return rough - (LEARN_RATE * ATAN_SCALE) * turn, nm, nv


def backward_kernel(
    after_ref, ya_ref, yb_ref, yw_ref, rs_ref, scr, shifted, across, lr_ref, m_ref, v_ref,
    nr_ref, nm_ref, nv_ref, ml_ref, mr_ref, g_ref, row_s, row_scr, row_sh, row_ac, row_g,
):
    gy, ny = place("gy")
    even_y, at_wall_y = gy % 2 == 0, (gy == 0) | (gy == ny - 1)
    height, lanes = lr_ref.shape

    def put_grad(j, value):
        g_ref[rows(j), :] = value

    third_pass(height // BLK, scr, shifted, across, put_grad)
    for f in range(NF):
        r = slice(3 * f, 3 * f + 3)
        ya, yb = ya_ref[r, :], jnp.where(at_wall_y, yw_ref[r, :], yb_ref[r, :])
        row_s[f, 0:8, :] = jnp.ones((8, lanes), jnp.float32)
        row_s[f, 24:32, :] = jnp.ones((8, lanes), jnp.float32)
        row_s[f, 5:8, :] = jnp.where(even_y, yb, ya)
        row_s[f, 24:27, :] = jnp.where(even_y, ya, yb)
        row_s[f, 8:24, :] = rs_ref[f]
    strip_gradient(row_s, row_scr, row_sh, row_ac, row_g)
    row = lax.broadcasted_iota(jnp.int32, (8, lanes), 0)
    g_ref[0:8, :] = jnp.where(row < 3, row_g[8:16, :], g_ref[0:8, :])
    g_ref[height - 8 : height, :] = jnp.where(row >= 5, row_g[16:24, :], g_ref[height - 8 : height, :])

    def update(j):
        r = rows(j)
        nr_ref[r, :], nm_ref[r, :], nv_ref[r, :] = updated(
            g_ref[r, :], lr_ref[r, :], m_ref[r, :], v_ref[r, :]
        )

    looped(height // BLK, update)
    lane = lax.broadcasted_iota(jnp.int32, (height, 128), 1)
    for f, ref in enumerate((m_ref, v_ref)):
        turned = jnp.where(lane < 64, ref[:, 0:128], ref[:, lanes - 128 : lanes]).T
        ml_ref[f] = turned[0:8, :]
        mr_ref[f] = turned[120:128, :]


def pack_cols_kernel(yb_ref, ya_ref, yw_ref, tl_ref, tr_ref, b_ref, a_ref, pl_ref, pr_ref, k_scr):
    gx, nx = place("gx")
    gy, ny = place("gy")
    even_y = gy % 2 == 0
    lanes = ya_ref.shape[1]
    y_b = jnp.where((gy == 0) | (gy == ny - 1), yw_ref[...], yb_ref[...])
    below = jnp.where(even_y, ya_ref[...], y_b)
    above = jnp.where(even_y, y_b, ya_ref[...])
    lane = lax.broadcasted_iota(jnp.int32, (above.shape[0], 128), 1)
    above = jnp.where(lane < 64, above[:, 0:128], above[:, lanes - 128 : lanes])
    below = jnp.where(lane < 64, below[:, 0:128], below[:, lanes - 128 : lanes])
    k_scr[...] = jnp.zeros_like(k_scr)
    for f in range(NF):
        k_scr[6 * f : 6 * f + 3, :] = above[3 * f : 3 * f + 3, :]
        k_scr[6 * f + 3 : 6 * f + 6, :] = below[3 * f : 3 * f + 3, :]
    turned = k_scr[...].T
    left_corner, right_corner = turned[0:8, :], turned[120:128, :]
    pl_ref[...] = left_corner
    pr_ref[...] = right_corner
    even = gx % 2 == 0
    a_ref[...] = jnp.zeros_like(a_ref)
    b_ref[...] = jnp.zeros_like(b_ref)
    first, last = gx == 0, gx == nx - 1
    for f in range(NF):
        sign = -1.0 if f in (QX, CX) else 1.0
        t = three_rows(tl_ref[f], 0, first, sign)
        b = three_rows(tr_ref[f], 5, last, sign)
        a_ref[3 * f : 3 * f + 3, :] = jnp.where(even, b, t)
        b_ref[3 * f : 3 * f + 3, :] = jnp.where(even, t, b)
    lane = lax.broadcasted_iota(jnp.int32, (3, 128), 1)
    flip = ((lane >= 6 * QX) & (lane < 6 * QX + 6)) | ((lane >= 6 * CX) & (lane < 6 * CX + 6))
    sign = jnp.where(flip, -1.0, 1.0)
    t = three_rows(left_corner, 0, first, sign)
    b = three_rows(right_corner, 5, last, sign)
    a_ref[32:35, 0:128] = jnp.where(even, b, t)
    b_ref[32:35, 0:128] = jnp.where(even, t, b)


def rim_kernel(
    xa_ref, xb_ref, xw_ref, tl_ref, tr_ref, pl_ref, pr_ref, ml_ref, mr_ref, ir_ref, im_ref, iv_ref,
    nr_ref, nm_ref, nv_ref, col_s, col_scr, col_sh, col_ac, col_g, turn_scr,
):
    gx, nx = place("gx")
    even_x, at_wall_x = gx % 2 == 0, (gx == 0) | (gx == nx - 1)
    height, lanes = ir_ref.shape
    x_b = jnp.where(at_wall_x, xw_ref[...], xb_ref[...])
    left_in = jnp.where(even_x, x_b, xa_ref[...])
    right_in = jnp.where(even_x, xa_ref[...], x_b)
    for f, t in enumerate(TURNED):
        shift = (125 - 6 * f) % 128
        r = slice(3 * f, 3 * f + 3)
        col_s[t, 0:8, :] = jnp.ones((8, height + 128), jnp.float32)
        col_s[t, 24:32, :] = jnp.ones((8, height + 128), jnp.float32)
        col_s[t, 5:8, 0:height] = left_in[r, :]
        col_s[t, 24:27, 0:height] = right_in[r, :]
        col_s[t, 8:16, 0:height] = tl_ref[f]
        col_s[t, 16:24, 0:height] = tr_ref[f]
        col_s[t, 5:8, height:] = pltpu.roll(left_in[32:40, 0:128], shift, 1)[0:3, :]
        col_s[t, 24:27, height:] = pltpu.roll(right_in[32:40, 0:128], shift, 1)[0:3, :]
        col_s[t, 8:16, height:] = pltpu.roll(pl_ref[...], shift, 1)
        col_s[t, 16:24, height:] = pltpu.roll(pr_ref[...], shift, 1)
    strip_gradient(col_s, col_scr, col_sh, col_ac, col_g)
    turn_scr[:, 8:120, :] = jnp.zeros((3, 112, height), jnp.float32)
    for r, g, t_ref, s_ref in ((slice(0, 8), 8, tl_ref, ml_ref), (slice(120, 128), 16, tr_ref, mr_ref)):
        new = updated(col_g[g : g + 8, 0:height], t_ref[LR], s_ref[0], s_ref[1])
        for f in range(3):
            turn_scr[f, r, :] = new[f]
    lane = lax.broadcasted_iota(jnp.int32, (height, 128), 1)
    for f, (src, dst) in enumerate(((ir_ref, nr_ref), (im_ref, nm_ref), (iv_ref, nv_ref))):
        side = turn_scr[f].T
        dst[:, 0:128] = jnp.where(lane < 3, side, src[:, 0:128])
        dst[:, lanes - 128 : lanes] = jnp.where(lane >= 125, side, src[:, lanes - 128 : lanes])


def swap_pairs(nx, ny, axis, odd):
    pairs = []
    for x in range(nx):
        for y in range(ny):
            u, v = x, y
            if axis == "gx":
                u = x ^ 1 if not odd else ((x + 1) ^ 1) - 1
                if not 0 <= u < nx:
                    u, v = x, y ^ 1
            else:
                v = y ^ 1 if not odd else ((y + 1) ^ 1) - 1
                if not 0 <= v < ny:
                    u, v = x ^ 1, y
            pairs.append((x * ny + y, u * ny + v))
    return pairs


def swapped(value, axis, odd):
    pairs = swap_pairs(lax.axis_size("gx"), lax.axis_size("gy"), axis, odd)
    return lax.ppermute(value, ("gx", "gy"), pairs)


def call(kernel, out_shapes, scratch=(), in_specs=None, flops=0, vmem_mb=VMEM_MB):
    params = pltpu.CompilerParams(vmem_limit_bytes=vmem_mb << 20)
    shapes = [jax.ShapeDtypeStruct(s, jnp.float32) for s in out_shapes]
    kwargs = {} if in_specs is None else {"in_specs": in_specs}
    return pl.pallas_call(
        kernel,
        out_shape=shapes,
        scratch_shapes=list(scratch),
        compiler_params=params,
        cost_estimate=pl.CostEstimate(flops=flops, bytes_accessed=flops // 8, transcendentals=0),
        **kwargs,
    )


def on_device(water, ground, rough, moment, second, wet_tiles, cot):
    height, lanes = ground.shape
    hbm = pl.BlockSpec(memory_space=pltpu.HBM)
    y_b, y_a, wet = call(
        pack_rows_kernel,
        [(32, lanes), (32, lanes), (16, lanes)],
        scratch=[
            pltpu.SMEM((2, 2), jnp.int32),
            pltpu.VMEM((8, 8, lanes), jnp.float32),
            pltpu.VMEM((8, 8, lanes), jnp.float32),
            pltpu.SemaphoreType.DMA((9,)),
        ],
        in_specs=[hbm] * 5,
        vmem_mb=12,
    )(*(pltpu.with_memory_space_constraint(x, pltpu.HBM) for x in (wet_tiles, water, ground, rough, cot)))
    y_wall, y_b, y_a = y_b, swapped(y_b, "gy", True), swapped(y_a, "gy", False)
    kept = [
        (N_AHEAD, height, lanes),
        (N_SHIFTED, lanes // 128, height + 16, 128),
        (N_ACROSS, height, lanes),
    ]
    scr, shifted, across, row_own, col_left, col_right = call(
        forward_kernel, [*kept, (NF, 16, lanes), (NF, 8, height), (NF, 8, height)], flops=20_000_000
    )(wet, water, ground, rough, cot)
    x_b, x_a, corner_left, corner_right = call(
        pack_cols_kernel,
        [(40, height), (40, height), (8, 128), (8, 128)],
        scratch=[pltpu.VMEM((128, 128), jnp.float32)],
    )(y_b, y_a, y_wall, col_left, col_right)
    own_rough, own_moment, own_second, mom_left, mom_right = call(
        backward_kernel,
        [(height, lanes)] * 3 + [(2, 8, height)] * 2,
        scratch=[
            pltpu.VMEM((height, lanes), jnp.float32),
            pltpu.VMEM((NF, 32, lanes), jnp.float32),
            pltpu.VMEM((N_AHEAD, 32, lanes), jnp.float32),
            pltpu.VMEM((N_SHIFTED, lanes // 128, 48, 128), jnp.float32),
            pltpu.VMEM((N_ACROSS, 32, lanes), jnp.float32),
            pltpu.VMEM((32, lanes), jnp.float32),
        ],
        flops=20_000_000,
    )(corner_left, y_a, y_b, y_wall, row_own, scr, shifted, across, rough, moment, second)
    x_wall, x_b, x_a = x_b, swapped(x_b, "gx", True), swapped(x_a, "gx", False)
    return tuple(
        call(
            rim_kernel,
            [(height, lanes)] * 3,
            scratch=[
                pltpu.VMEM((NF, 32, height + 128), jnp.float32),
                pltpu.VMEM((N_AHEAD, 32, height + 128), jnp.float32),
                pltpu.VMEM((N_SHIFTED, height // 128 + 1, 48, 128), jnp.float32),
                pltpu.VMEM((N_ACROSS, 32, height + 128), jnp.float32),
                pltpu.VMEM((32, height + 128), jnp.float32),
                pltpu.VMEM((3, 128, height), jnp.float32),
            ],
        )(
            x_a, x_b, x_wall, col_left, col_right, corner_left, corner_right,
            mom_left, mom_right, own_rough, own_moment, own_second,
        )
    )


def solution(mesh):
    flat = P("gy", "gx")
    deep = P(None, "gy", "gx")

    return jax.shard_map(
        on_device,
        mesh=mesh,
        in_specs=(deep, flat, flat, flat, flat, flat, deep),
        out_specs=(flat, flat, flat),
        check_vma=False,
    )
```

```python
import math

import jax
import jax.numpy as jnp
from jax import lax
from jax.experimental import pallas as pl
from jax.experimental.pallas import tpu as pltpu
from jax.sharding import PartitionSpec as P

UPDATES = 20
GRAVITY = 9.81
HALF_STEP = 0.05
LOG_DRAG = math.log(9.81)
SPEED_EPS = 0.0001
BETA_ONE = 0.9
BETA_TWO = 0.999
LEARN_RATE = 0.05
ATAN_SCALE = 1.27
H, QX, QY, Z, LR, CH, CX, CY, WET = range(9)
NF = 9
COUNT = (3, 3, 3, 3, 2, 1, 1, 1, 1)
START = (0, 3, 6, 9, 12, 14, 15, 16, 17)
SENT = 18
TURNED = (H, QY, QX, Z, LR, CH, CY, CX, WET)
BLK = 8
UNROLL = 8
VMEM_MB = 12


def from_prev_col(x):
    return pltpu.roll(x, 1, 1)


def from_next_col(x):
    return pltpu.roll(x, x.shape[1] - 1, 1)


def flux_parts(h, qx, qy, slope_x, slope_y):
    inv = 1.0 / h
    u, v = qx * inv, qy * inv
    press = (0.5 * GRAVITY) * h * h
    k = HALF_STEP
    fx1, fy1 = k * qx, k * qy
    fx2, fxy, fy3 = k * (qx * u + press), k * (qx * v), k * (qy * v + press)
    h4, x4, y4 = 0.25 * h, 0.25 * qx, 0.25 * qy
    cols = [
        from_prev_col(h4 + fx1) + from_next_col(h4 - fx1),
        from_prev_col(x4 + fx2) + from_next_col(x4 - fx2) - h * slope_x,
        from_prev_col(y4 + fxy) + from_next_col(y4 - fxy) - h * slope_y,
    ]
    down = [h4 + fy1, x4 + fxy, y4 + fy3]
    up = [h4 - fy1, x4 - fxy, y4 - fy3]
    return cols, down, up, u, v


def drag_parts(h, qx, qy, rough):
    s2 = qx * qx + qy * qy + SPEED_EPS
    rs = lax.rsqrt(s2)
    b = jnp.exp(2.0 * rough + LOG_DRAG - (7.0 / 3.0) * jnp.log(h)) * (s2 * rs)
    w = 1.0 / (1.0 + b)
    return b, w, rs * rs


def rows(j):
    if isinstance(j, int):
        return slice(j * BLK, j * BLK + BLK)
    return pl.ds(pl.multiple_of(j * BLK, BLK), BLK)


def take(ref, j, off=0):
    r = pl.ds(j * BLK + 8 + off, BLK)
    if off == 0 and not isinstance(j, int):
        r = pl.ds(pl.multiple_of(j * BLK + 8, 8), BLK)
    return jnp.concatenate([ref[t, r, :] for t in range(ref.shape[0])], 1)


def give(ref, j, value):
    put(ref, pl.ds(pl.multiple_of(j * BLK + 8, 8), BLK), value)


def put(ref, r, value, at=0):
    for t in range(value.shape[1] // 128):
        ref[at + t, r, :] = value[:, 128 * t : 128 * t + 128]


def looped(n, step):
    if n <= 8:
        for j in range(n):
            step(j)
        return

    def body(j, carry):
        step(j)
        return carry

    lax.fori_loop(0, n, body, 0, unroll=UNROLL)


UH, UX, UY, SX, SY, GA, GB = range(7)
N_AHEAD, N_ACROSS, N_SHIFTED = 7, 5, 6
DOWN, UP = 0, 3
PH, PX, PY = range(3)
VU, VV = 3, 4


def gathered(shifted, across, j):
    r = rows(j)
    return [
        take(shifted.at[DOWN + f], j, -1) + take(shifted.at[UP + f], j, 1) + across[f, r, :]
        for f in range(3)
    ]


def first_pass(get, wet, n, scr, shifted, across, adj):
    zs = adj.at[0]
    looped(n, lambda j: give(zs, j, get(Z, j)))

    def parts(j):
        r = rows(j)
        kg = HALF_STEP * GRAVITY
        z = get(Z, j)
        sx = kg * (from_next_col(z) - from_prev_col(z))
        sy = kg * (take(zs, j, 1) - take(zs, j, -1))
        scr[SX, r, :] = sx
        scr[SY, r, :] = sy
        cols, down, up, _, _ = flux_parts(get(H, j), get(QX, j), get(QY, j), sx, sy)
        for f in range(3):
            across[f, r, :] = cols[f]
            give(shifted.at[DOWN + f], j, down[f])
            give(shifted.at[UP + f], j, up[f])

    looped(n, parts)

    def finish(j):
        r = rows(j)
        h, qx, qy = gathered(shifted, across, j)
        b, w, _ = drag_parts(h, qx, qy, get(LR, j))
        m = wet(j)
        scr[UH, r, :] = jnp.where(m, h, get(H, j))
        scr[UX, r, :] = jnp.where(m, qx * w, get(QX, j))
        scr[UY, r, :] = jnp.where(m, qy * w, get(QY, j))
        t = jnp.where(m, -2.0 * b * w * w, 0.0)
        scr[GA, r, :] = t * qx
        scr[GB, r, :] = t * qy

    looped(n, finish)


def second_pass(get, wet, n, scr, shifted, across, adj, pg):
    def parts(j):
        r = rows(j)
        cols, down, up, u, v = flux_parts(*(scr[f, r, :] for f in (UH, UX, UY, SX, SY)))
        across[VU, r, :] = u
        across[VV, r, :] = v
        for f in range(3):
            across[f, r, :] = cols[f]
            give(shifted.at[DOWN + f], j, down[f])
            give(shifted.at[UP + f], j, up[f])

    looped(n, parts)

    def finish(j):
        h, qx, qy = gathered(shifted, across, j)
        b, w, inv_s2 = drag_parts(h, qx, qy, get(LR, j))
        m = wet(j)
        ch, cx, cy = get(CH, j), get(CX, j), get(CY, j)
        t = (cx * qx + cy * qy) * (w * w) * b
        ts = t * inv_s2
        return [
            jnp.where(m, ch + (7.0 / 3.0) * t / h, 0.0),
            jnp.where(m, cx * w - ts * qx, 0.0),
            jnp.where(m, cy * w - ts * qy, 0.0),
            jnp.where(m, -2.0 * t, 0.0),
        ]

    def finish_all(j):
        for f, value in enumerate(finish(j)):
            if f < 3:
                give(adj.at[f], j, value)
            else:
                pg[rows(j), :] = value

    looped(n, finish_all)


def third_pass(blocks, scr, across, adj, pg, put_grad):
    def back(j):
        r = rows(j)

        def four(f):
            ref = adj.at[f]
            cur = take(ref, j)
            return from_next_col(cur), from_prev_col(cur), take(ref, j, 1), take(ref, j, -1)

        he, hw, hs, hn = four(PH)
        xe, xw, xs, xn = four(PX)
        ye, yw, ys, yn = four(PY)
        u, v = across[VU, r, :], across[VV, r, :]
        k = HALF_STEP
        cross = k * ((ye - yw) + (xs - xn))
        cot_x = (
            0.25 * ((xe + xw) + (xs + xn))
            + k * (he - hw)
            + (2.0 * k) * u * (xe - xw)
            + v * cross
        )
        cot_y = (
            0.25 * ((ye + yw) + (ys + yn))
            + k * (hs - hn)
            + (2.0 * k) * v * (ys - yn)
            + u * cross
        )
        put_grad(j, pg[r, :] + scr[GA, r, :] * cot_x + scr[GB, r, :] * cot_y)

    if isinstance(blocks, int):
        looped(blocks, back)
    else:
        for j in blocks:
            back(j)


def place(axis):
    index = lax.axis_index(axis)
    return index, lax.axis_size(axis)


def top_rows(block, count, mirrored, sign):
    reverse = jnp.concatenate([block[d : d + 1, :] for d in reversed(range(count))], 0)
    return jnp.where(mirrored, sign * reverse, block[0:count, :])


def bottom_rows(block, count, mirrored, sign):
    reverse = jnp.concatenate([block[d : d + 1, :] for d in range(7, 7 - count, -1)], 0)
    return jnp.where(mirrored, sign * reverse, block[8 - count : 8, :])


def sent(f):
    return slice(START[f], START[f] + COUNT[f])


def pack_rows_kernel(wet_hbm, w_hbm, z_hbm, lr_hbm, c_hbm, b_ref, a_ref, wet_ref, wet_s, top, bot, sems):
    height, lanes = z_hbm.shape
    copies = [pltpu.make_async_copy(wet_hbm, wet_s, sems.at[0])]
    for side, (buf, row) in enumerate(((top, 0), (bot, height - 8))):
        r = pl.ds(row, 8)
        for at, (src, dst) in enumerate((
            (w_hbm.at[:, r, :], buf.at[pl.ds(0, 3)]),
            (z_hbm.at[r, :], buf.at[Z]),
            (lr_hbm.at[r, :], buf.at[LR]),
            (c_hbm.at[:, r, :], buf.at[pl.ds(CH, 3)]),
        )):
            copies.append(pltpu.make_async_copy(src, dst, sems.at[1 + 4 * side + at]))
    for copy in copies:
        copy.start()
    gy, ny = place("gy")
    even = gy % 2 == 0
    lane = lax.broadcasted_iota(jnp.int32, (8, lanes), 1)
    a_ref[16:24, :] = jnp.zeros((8, lanes), jnp.float32)
    b_ref[16:24, :] = jnp.zeros((8, lanes), jnp.float32)
    for copy in copies:
        copy.wait()
    for row in range(2):
        left = (wet_s[row, 0] > 0).astype(jnp.float32)
        right = (wet_s[row, 1] > 0).astype(jnp.float32)
        wet_ref[8 * row : 8 * row + 8, :] = jnp.where(lane < lanes // 2, left, right)
    for f in range(NF):
        sign = -1.0 if f in (QY, CY) else 1.0
        t = top_rows(top[f] if f < WET else wet_ref[0:8, :], COUNT[f], gy == 0, sign)
        b = bottom_rows(bot[f] if f < WET else wet_ref[8:16, :], COUNT[f], gy == ny - 1, sign)
        a_ref[sent(f), :] = jnp.where(even, b, t)
        b_ref[sent(f), :] = jnp.where(even, t, b)


def tile_wet(wet_ref, j, n):
    return wet_ref[rows(j // (n // 2)), :] > 0.5


def forward_kernel(wet_ref, w_ref, z_ref, lr_ref, c_ref, scr, across, adj, pg, rs_ref, tl_ref, tr_ref, shifted):
    height, lanes = z_ref.shape
    n = height // BLK

    def field(f):
        if f <= QY:
            return w_ref.at[f]
        return z_ref if f == Z else lr_ref if f == LR else c_ref.at[f - CH]

    def get(f, j):
        return field(f)[rows(j), :]

    first_pass(get, lambda j: tile_wet(wet_ref, j, n), n, scr, shifted, across, adj)
    second_pass(get, lambda j: tile_wet(wet_ref, j, n), n, scr, shifted, across, adj, pg)
    lane = lax.broadcasted_iota(jnp.int32, (height, 128), 1)
    for f in range(WET):
        ref = field(f)
        rs_ref[f, 0:8, :] = ref[0:8, :]
        rs_ref[f, 8:16, :] = ref[height - 8 : height, :]
        turned = jnp.where(lane < 64, ref[:, 0:128], ref[:, lanes - 128 : lanes]).T
        tl_ref[f] = turned[0:8, :]
        tr_ref[f] = turned[120:128, :]
    top, bottom = wet_ref[0:8, :], wet_ref[8:16, :]
    rs_ref[WET, 0:8, :] = top
    rs_ref[WET, 8:16, :] = bottom
    half = lanes // 2
    tl_ref[WET] = jnp.concatenate([top[:, :half], bottom[:, :half]], 1)
    tr_ref[WET] = jnp.concatenate([top[:, half:], bottom[:, half:]], 1)


def strip_gradient(s_ref, scr, shifted, across, adj, pg, g_ref):
    n = s_ref.shape[1] // BLK

    def get(f, j):
        return s_ref[f, rows(j), :]

    def wet(j):
        return get(WET, j) > 0.5

    def put_grad(j, value):
        g_ref[rows(j), :] = value

    first_pass(get, wet, n, scr, shifted, across, adj)
    second_pass(get, wet, n, scr, shifted, across, adj, pg)
    third_pass((1, 2), scr, across, adj, pg, put_grad)


def arctan_ratio(y, x):
    a = jnp.abs(y)
    big, small = jnp.maximum(a, x), jnp.minimum(a, x)
    far = small > 0.41421356 * big
    t = jnp.where(far, small - big, small) / jnp.where(far, small + big, big)
    z = t * t
    p = ((8.05374449538e-2 * z - 1.38776856032e-1) * z + 1.99777106478e-1) * z - 3.33329491539e-1
    r = p * z * t + t + jnp.where(far, math.pi / 4, 0.0)
    r = jnp.where(a > x, math.pi / 2 - r, r)
    return jnp.where(y < 0, -r, r)


def updated(g, rough, moment, second):
    nm = BETA_ONE * moment + (1.0 - BETA_ONE) * g
    nv = BETA_TWO * second + (1.0 - BETA_TWO) * g * g
    root = jnp.sqrt(nv * (1.0 / (1.0 - BETA_TWO**UPDATES)))
    turn = arctan_ratio(nm * (1.0 / (1.0 - BETA_ONE**UPDATES)), root)
    return rough - (LEARN_RATE * ATAN_SCALE) * turn, nm, nv


def backward_kernel(
    after_ref, ya_ref, yb_ref, yw_ref, rs_ref, scr, across, adj, pg, lr_ref, m_ref, v_ref,
    nr_ref, nm_ref, nv_ref, ml_ref, mr_ref, g_ref, row_s, row_scr, row_sh, row_ac, row_adj, row_pg, row_g,
):
    gy, ny = place("gy")
    even_y, at_wall_y = gy % 2 == 0, (gy == 0) | (gy == ny - 1)
    height, lanes = lr_ref.shape

    def put_grad(j, value):
        g_ref[rows(j), :] = value

    third_pass(height // BLK, scr, across, adj, pg, put_grad)
    for f in range(NF):
        r, c = sent(f), COUNT[f]
        ya, yb = ya_ref[r, :], jnp.where(at_wall_y, yw_ref[r, :], yb_ref[r, :])
        row_s[f, 0:8, :] = jnp.ones((8, lanes), jnp.float32)
        row_s[f, 24:32, :] = jnp.ones((8, lanes), jnp.float32)
        row_s[f, 8 - c : 8, :] = jnp.where(even_y, yb, ya)
        row_s[f, 24 : 24 + c, :] = jnp.where(even_y, ya, yb)
        row_s[f, 8:24, :] = rs_ref[f]
    strip_gradient(row_s, row_scr, row_sh, row_ac, row_adj, row_pg, row_g)
    row = lax.broadcasted_iota(jnp.int32, (8, lanes), 0)
    g_ref[0:8, :] = jnp.where(row < 3, row_g[8:16, :], g_ref[0:8, :])
    g_ref[height - 8 : height, :] = jnp.where(row >= 5, row_g[16:24, :], g_ref[height - 8 : height, :])

    def update(j):
        r = rows(j)
        nr_ref[r, :], nm_ref[r, :], nv_ref[r, :] = updated(
            g_ref[r, :], lr_ref[r, :], m_ref[r, :], v_ref[r, :]
        )

    looped(height // BLK, update)
    lane = lax.broadcasted_iota(jnp.int32, (height, 128), 1)
    for f, ref in enumerate((m_ref, v_ref)):
        turned = jnp.where(lane < 64, ref[:, 0:128], ref[:, lanes - 128 : lanes]).T
        ml_ref[f] = turned[0:8, :]
        mr_ref[f] = turned[120:128, :]


def pack_cols_kernel(yb_ref, ya_ref, yw_ref, tl_ref, tr_ref, b_ref, a_ref, pl_ref, pr_ref, k_scr):
    gx, nx = place("gx")
    gy, ny = place("gy")
    even_y = gy % 2 == 0
    lanes = ya_ref.shape[1]
    y_b = jnp.where((gy == 0) | (gy == ny - 1), yw_ref[...], yb_ref[...])
    below = jnp.where(even_y, ya_ref[...], y_b)
    above = jnp.where(even_y, y_b, ya_ref[...])
    lane = lax.broadcasted_iota(jnp.int32, (above.shape[0], 128), 1)
    above = jnp.where(lane < 64, above[:, 0:128], above[:, lanes - 128 : lanes])
    below = jnp.where(lane < 64, below[:, 0:128], below[:, lanes - 128 : lanes])
    k_scr[...] = jnp.zeros_like(k_scr)
    for f in range(NF):
        c = 3 if f == WET else COUNT[f]
        k_scr[6 * f + 3 - c : 6 * f + 3, :] = jnp.broadcast_to(above[sent(f), :], (c, 128))
        k_scr[6 * f + 3 : 6 * f + 3 + c, :] = jnp.broadcast_to(below[sent(f), :], (c, 128))
    turned = k_scr[...].T
    left_corner, right_corner = turned[0:8, :], turned[120:128, :]
    pl_ref[...] = left_corner
    pr_ref[...] = right_corner
    even = gx % 2 == 0
    a_ref[...] = jnp.zeros_like(a_ref)
    b_ref[...] = jnp.zeros_like(b_ref)
    first, last = gx == 0, gx == nx - 1
    for f in range(NF):
        sign = -1.0 if f in (QX, CX) else 1.0
        t = top_rows(tl_ref[f], COUNT[f], first, sign)
        b = bottom_rows(tr_ref[f], COUNT[f], last, sign)
        a_ref[sent(f), :] = jnp.where(even, b, t)
        b_ref[sent(f), :] = jnp.where(even, t, b)
    lane = lax.broadcasted_iota(jnp.int32, (3, 128), 1)
    flip = ((lane >= 6 * QX) & (lane < 6 * QX + 6)) | ((lane >= 6 * CX) & (lane < 6 * CX + 6))
    sign = jnp.where(flip, -1.0, 1.0)
    t = top_rows(left_corner, 3, first, sign)
    b = bottom_rows(right_corner, 3, last, sign)
    a_ref[SENT : SENT + 3, 0:128] = jnp.where(even, b, t)
    b_ref[SENT : SENT + 3, 0:128] = jnp.where(even, t, b)


def rim_kernel(
    xa_ref, xb_ref, xw_ref, tl_ref, tr_ref, pl_ref, pr_ref, ml_ref, mr_ref, ir_ref, im_ref, iv_ref,
    nr_ref, nm_ref, nv_ref, col_s, col_scr, col_sh, col_ac, col_adj, col_pg, col_g, turn_scr,
):
    gx, nx = place("gx")
    even_x, at_wall_x = gx % 2 == 0, (gx == 0) | (gx == nx - 1)
    height, lanes = ir_ref.shape
    x_b = jnp.where(at_wall_x, xw_ref[...], xb_ref[...])
    left_in = jnp.where(even_x, x_b, xa_ref[...])
    right_in = jnp.where(even_x, xa_ref[...], x_b)
    for f, t in enumerate(TURNED):
        shift = (125 - 6 * f) % 128
        r, c = sent(f), COUNT[f]
        col_s[t, 0:8, :] = jnp.ones((8, height + 128), jnp.float32)
        col_s[t, 24:32, :] = jnp.ones((8, height + 128), jnp.float32)
        col_s[t, 8 - c : 8, 0:height] = left_in[r, :]
        col_s[t, 24 : 24 + c, 0:height] = right_in[r, :]
        col_s[t, 8:16, 0:height] = tl_ref[f]
        col_s[t, 16:24, 0:height] = tr_ref[f]
        col_s[t, 5:8, height:] = pltpu.roll(left_in[16:24, 0:128], shift, 1)[2:5, :]
        col_s[t, 24:27, height:] = pltpu.roll(right_in[16:24, 0:128], shift, 1)[2:5, :]
        col_s[t, 8:16, height:] = pltpu.roll(pl_ref[...], shift, 1)
        col_s[t, 16:24, height:] = pltpu.roll(pr_ref[...], shift, 1)
    strip_gradient(col_s, col_scr, col_sh, col_ac, col_adj, col_pg, col_g)
    turn_scr[:, 8:120, :] = jnp.zeros((3, 112, height), jnp.float32)
    for r, g, t_ref, s_ref in ((slice(0, 8), 8, tl_ref, ml_ref), (slice(120, 128), 16, tr_ref, mr_ref)):
        new = updated(col_g[g : g + 8, 0:height], t_ref[LR], s_ref[0], s_ref[1])
        for f in range(3):
            turn_scr[f, r, :] = new[f]
    lane = lax.broadcasted_iota(jnp.int32, (height, 128), 1)
    for f, (src, dst) in enumerate(((ir_ref, nr_ref), (im_ref, nm_ref), (iv_ref, nv_ref))):
        side = turn_scr[f].T
        dst[:, 0:128] = jnp.where(lane < 3, side, src[:, 0:128])
        dst[:, lanes - 128 : lanes] = jnp.where(lane >= 125, side, src[:, lanes - 128 : lanes])


def swap_pairs(nx, ny, axis, odd):
    pairs = []
    for x in range(nx):
        for y in range(ny):
            u, v = x, y
            if axis == "gx":
                u = x ^ 1 if not odd else ((x + 1) ^ 1) - 1
                if not 0 <= u < nx:
                    u, v = x, y ^ 1
            else:
                v = y ^ 1 if not odd else ((y + 1) ^ 1) - 1
                if not 0 <= v < ny:
                    u, v = x ^ 1, y
            pairs.append((x * ny + y, u * ny + v))
    return pairs


def swapped(value, axis, odd):
    pairs = swap_pairs(lax.axis_size("gx"), lax.axis_size("gy"), axis, odd)
    return lax.ppermute(value, ("gx", "gy"), pairs)


def call(kernel, out_shapes, scratch=(), in_specs=None, flops=0, vmem_mb=VMEM_MB):
    params = pltpu.CompilerParams(vmem_limit_bytes=vmem_mb << 20)
    shapes = [jax.ShapeDtypeStruct(s, jnp.float32) for s in out_shapes]
    kwargs = {} if in_specs is None else {"in_specs": in_specs}
    return pl.pallas_call(
        kernel,
        out_shape=shapes,
        scratch_shapes=list(scratch),
        compiler_params=params,
        cost_estimate=pl.CostEstimate(flops=flops, bytes_accessed=flops // 8, transcendentals=0),
        **kwargs,
    )


def on_device(water, ground, rough, moment, second, wet_tiles, cot):
    height, lanes = ground.shape
    hbm = pl.BlockSpec(memory_space=pltpu.HBM)
    y_b, y_a, wet = call(
        pack_rows_kernel,
        [(24, lanes), (24, lanes), (16, lanes)],
        scratch=[
            pltpu.SMEM((2, 2), jnp.int32),
            pltpu.VMEM((8, 8, lanes), jnp.float32),
            pltpu.VMEM((8, 8, lanes), jnp.float32),
            pltpu.SemaphoreType.DMA((9,)),
        ],
        in_specs=[hbm] * 5,
        vmem_mb=12,
    )(*(pltpu.with_memory_space_constraint(x, pltpu.HBM) for x in (wet_tiles, water, ground, rough, cot)))
    y_wall, y_b, y_a = y_b, swapped(y_b, "gy", True), swapped(y_a, "gy", False)
    kept = [
        (N_AHEAD, height, lanes),
        (N_ACROSS, height, lanes),
        (3, lanes // 128, height + 16, 128),
        (height, lanes),
    ]
    scr, across, adj, pg, row_own, col_left, col_right = call(
        forward_kernel,
        [*kept, (NF, 16, lanes), (NF, 8, height), (NF, 8, height)],
        scratch=[pltpu.VMEM((N_SHIFTED, lanes // 128, height + 16, 128), jnp.float32)],
        flops=20_000_000,
    )(wet, water, ground, rough, cot)
    x_b, x_a, corner_left, corner_right = call(
        pack_cols_kernel,
        [(24, height), (24, height), (8, 128), (8, 128)],
        scratch=[pltpu.VMEM((128, 128), jnp.float32)],
    )(y_b, y_a, y_wall, col_left, col_right)
    own_rough, own_moment, own_second, mom_left, mom_right = call(
        backward_kernel,
        [(height, lanes)] * 3 + [(2, 8, height)] * 2,
        scratch=[
            pltpu.VMEM((height, lanes), jnp.float32),
            pltpu.VMEM((NF, 32, lanes), jnp.float32),
            pltpu.VMEM((N_AHEAD, 32, lanes), jnp.float32),
            pltpu.VMEM((N_SHIFTED, lanes // 128, 48, 128), jnp.float32),
            pltpu.VMEM((N_ACROSS, 32, lanes), jnp.float32),
            pltpu.VMEM((3, lanes // 128, 48, 128), jnp.float32),
            pltpu.VMEM((32, lanes), jnp.float32),
            pltpu.VMEM((32, lanes), jnp.float32),
        ],
        flops=20_000_000,
    )(corner_left, y_a, y_b, y_wall, row_own, scr, across, adj, pg, rough, moment, second)
    x_wall, x_b, x_a = x_b, swapped(x_b, "gx", True), swapped(x_a, "gx", False)
    return tuple(
        call(
            rim_kernel,
            [(height, lanes)] * 3,
            scratch=[
                pltpu.VMEM((NF, 32, height + 128), jnp.float32),
                pltpu.VMEM((N_AHEAD, 32, height + 128), jnp.float32),
                pltpu.VMEM((N_SHIFTED, height // 128 + 1, 48, 128), jnp.float32),
                pltpu.VMEM((N_ACROSS, 32, height + 128), jnp.float32),
                pltpu.VMEM((3, height // 128 + 1, 48, 128), jnp.float32),
                pltpu.VMEM((32, height + 128), jnp.float32),
                pltpu.VMEM((32, height + 128), jnp.float32),
                pltpu.VMEM((3, 128, height), jnp.float32),
            ],
        )(
            x_a, x_b, x_wall, col_left, col_right, corner_left, corner_right,
            mom_left, mom_right, own_rough, own_moment, own_second,
        )
    )


def solution(mesh):
    flat = P("gy", "gx")
    deep = P(None, "gy", "gx")

    return jax.shard_map(
        on_device,
        mesh=mesh,
        in_specs=(deep, flat, flat, flat, flat, flat, deep),
        out_specs=(flat, flat, flat),
        check_vma=False,
    )
```

```python
import math

import jax
import jax.numpy as jnp
from jax import lax
from jax.experimental import pallas as pl
from jax.experimental.pallas import tpu as pltpu
from jax.sharding import PartitionSpec as P

UPDATES = 20
GRAVITY = 9.81
HALF_STEP = 0.05
LOG_DRAG = math.log(9.81)
SPEED_EPS = 0.0001
BETA_ONE = 0.9
BETA_TWO = 0.999
LEARN_RATE = 0.05
ATAN_SCALE = 1.27
H, QX, QY, Z, LR, CH, CX, CY, WET = range(9)
NF = 9
COUNT = (3, 3, 3, 3, 2, 1, 1, 1, 1)
START = (0, 3, 6, 9, 12, 14, 15, 16, 17)
SENT = 18
TURNED = (H, QY, QX, Z, LR, CH, CY, CX, WET)
BLK = 8
UNROLL = 8
VMEM_MB = 16


def from_prev_col(x):
    return pltpu.roll(x, 1, 1)


def from_next_col(x):
    return pltpu.roll(x, x.shape[1] - 1, 1)


def flux_parts(h, qx, qy, slope_x, slope_y):
    inv = 1.0 / h
    u, v = qx * inv, qy * inv
    press = (0.5 * GRAVITY) * h * h
    k = HALF_STEP
    fx1, fy1 = k * qx, k * qy
    fx2, fxy, fy3 = k * (qx * u + press), k * (qx * v), k * (qy * v + press)
    h4, x4, y4 = 0.25 * h, 0.25 * qx, 0.25 * qy
    cols = [
        from_prev_col(h4 + fx1) + from_next_col(h4 - fx1),
        from_prev_col(x4 + fx2) + from_next_col(x4 - fx2) - h * slope_x,
        from_prev_col(y4 + fxy) + from_next_col(y4 - fxy) - h * slope_y,
    ]
    down = [h4 + fy1, x4 + fxy, y4 + fy3]
    up = [h4 - fy1, x4 - fxy, y4 - fy3]
    return cols, down, up, u, v


def drag_parts(h, qx, qy, rough):
    s2 = qx * qx + qy * qy + SPEED_EPS
    rs = lax.rsqrt(s2)
    b = jnp.exp(2.0 * rough + LOG_DRAG - (7.0 / 3.0) * jnp.log(h)) * (s2 * rs)
    w = 1.0 / (1.0 + b)
    return b, w, rs * rs


def rows(j):
    if isinstance(j, int):
        return slice(j * BLK, j * BLK + BLK)
    return pl.ds(pl.multiple_of(j * BLK, BLK), BLK)


def take(ref, j, off=0):
    r = pl.ds(j * BLK + 8 + off, BLK)
    if off == 0 and not isinstance(j, int):
        r = pl.ds(pl.multiple_of(j * BLK + 8, 8), BLK)
    return jnp.concatenate([ref[t, r, :] for t in range(ref.shape[0])], 1)


def give(ref, j, value):
    put(ref, pl.ds(pl.multiple_of(j * BLK + 8, 8), BLK), value)


def put(ref, r, value, at=0):
    for t in range(value.shape[1] // 128):
        ref[at + t, r, :] = value[:, 128 * t : 128 * t + 128]


def looped(n, step):
    if n <= 8:
        for j in range(n):
            step(j)
        return

    def body(j, carry):
        step(j)
        return carry

    lax.fori_loop(0, n, body, 0, unroll=UNROLL)


SX, SY, GA, GB = range(4)
N_AHEAD, N_ACROSS, N_SHIFTED = 4, 5, 6
DOWN, UP = 0, 3
PH, PX, PY = range(3)
VU, VV = 3, 4


def gathered(shifted, across, j):
    r = rows(j)
    return [
        take(shifted.at[DOWN + f], j, -1) + take(shifted.at[UP + f], j, 1) + across[f, r, :]
        for f in range(3)
    ]


def first_pass(get, wet, n, scr, shifted, across, adj, then):
    zs = adj.at[0]
    looped(n, lambda j: give(zs, j, get(Z, j)))

    def parts(j):
        r = rows(j)
        kg = HALF_STEP * GRAVITY
        z = get(Z, j)
        sx = kg * (from_next_col(z) - from_prev_col(z))
        sy = kg * (take(zs, j, 1) - take(zs, j, -1))
        scr[SX, r, :] = sx
        scr[SY, r, :] = sy
        cols, down, up, _, _ = flux_parts(get(H, j), get(QX, j), get(QY, j), sx, sy)
        for f in range(3):
            across[f, r, :] = cols[f]
            give(shifted.at[DOWN + f], j, down[f])
            give(shifted.at[UP + f], j, up[f])

    looped(n, parts)

    def finish(j):
        r = rows(j)
        h, qx, qy = gathered(shifted, across, j)
        b, w, _ = drag_parts(h, qx, qy, get(LR, j))
        m = wet(j)
        then(
            j,
            jnp.where(m, h, get(H, j)),
            jnp.where(m, qx * w, get(QX, j)),
            jnp.where(m, qy * w, get(QY, j)),
        )
        t = jnp.where(m, -2.0 * b * w * w, 0.0)
        scr[GA, r, :] = t * qx
        scr[GB, r, :] = t * qy

    looped(n, finish)


def second_parts(scr, shifted, across):
    def parts(j, h, qx, qy):
        r = rows(j)
        cols, down, up, u, v = flux_parts(h, qx, qy, scr[SX, r, :], scr[SY, r, :])
        across[VU, r, :] = u
        across[VV, r, :] = v
        for f in range(3):
            across[f, r, :] = cols[f]
            give(shifted.at[DOWN + f], j, down[f])
            give(shifted.at[UP + f], j, up[f])

    return parts


def second_pass(get, wet, n, shifted, across, adj, pg):
    def finish(j):
        h, qx, qy = gathered(shifted, across, j)
        b, w, inv_s2 = drag_parts(h, qx, qy, get(LR, j))
        m = wet(j)
        ch, cx, cy = get(CH, j), get(CX, j), get(CY, j)
        t = (cx * qx + cy * qy) * (w * w) * b
        ts = t * inv_s2
        return [
            jnp.where(m, ch + (7.0 / 3.0) * t / h, 0.0),
            jnp.where(m, cx * w - ts * qx, 0.0),
            jnp.where(m, cy * w - ts * qy, 0.0),
            jnp.where(m, -2.0 * t, 0.0),
        ]

    def finish_all(j):
        for f, value in enumerate(finish(j)):
            if f < 3:
                give(adj.at[f], j, value)
            else:
                pg[rows(j), :] = value

    looped(n, finish_all)


def third_pass(blocks, scr, across, adj, pg, put_grad):
    def back(j):
        r = rows(j)

        def four(f):
            ref = adj.at[f]
            cur = take(ref, j)
            return from_next_col(cur), from_prev_col(cur), take(ref, j, 1), take(ref, j, -1)

        he, hw, hs, hn = four(PH)
        xe, xw, xs, xn = four(PX)
        ye, yw, ys, yn = four(PY)
        u, v = across[VU, r, :], across[VV, r, :]
        k = HALF_STEP
        cross = k * ((ye - yw) + (xs - xn))
        cot_x = (
            0.25 * ((xe + xw) + (xs + xn))
            + k * (he - hw)
            + (2.0 * k) * u * (xe - xw)
            + v * cross
        )
        cot_y = (
            0.25 * ((ye + yw) + (ys + yn))
            + k * (hs - hn)
            + (2.0 * k) * v * (ys - yn)
            + u * cross
        )
        put_grad(j, pg[r, :] + scr[GA, r, :] * cot_x + scr[GB, r, :] * cot_y)

    if isinstance(blocks, int):
        looped(blocks, back)
    else:
        for j in blocks:
            back(j)


def place(axis):
    index = lax.axis_index(axis)
    return index, lax.axis_size(axis)


def top_rows(block, count, mirrored, sign):
    reverse = jnp.concatenate([block[d : d + 1, :] for d in reversed(range(count))], 0)
    return jnp.where(mirrored, sign * reverse, block[0:count, :])


def bottom_rows(block, count, mirrored, sign):
    reverse = jnp.concatenate([block[d : d + 1, :] for d in range(7, 7 - count, -1)], 0)
    return jnp.where(mirrored, sign * reverse, block[8 - count : 8, :])


def sent(f):
    return slice(START[f], START[f] + COUNT[f])


def pack_rows_kernel(wet_hbm, w_hbm, z_hbm, lr_hbm, c_hbm, b_ref, a_ref, wet_ref, wet_s, top, bot, sems):
    height, lanes = z_hbm.shape
    copies = [pltpu.make_async_copy(wet_hbm, wet_s, sems.at[0])]
    for side, (buf, row) in enumerate(((top, 0), (bot, height - 8))):
        r = pl.ds(row, 8)
        for at, (src, dst) in enumerate((
            (w_hbm.at[:, r, :], buf.at[pl.ds(0, 3)]),
            (z_hbm.at[r, :], buf.at[Z]),
            (lr_hbm.at[r, :], buf.at[LR]),
            (c_hbm.at[:, r, :], buf.at[pl.ds(CH, 3)]),
        )):
            copies.append(pltpu.make_async_copy(src, dst, sems.at[1 + 4 * side + at]))
    for copy in copies:
        copy.start()
    gy, ny = place("gy")
    even = gy % 2 == 0
    lane = lax.broadcasted_iota(jnp.int32, (8, lanes), 1)
    a_ref[16:24, :] = jnp.zeros((8, lanes), jnp.float32)
    b_ref[16:24, :] = jnp.zeros((8, lanes), jnp.float32)
    for copy in copies:
        copy.wait()
    for row in range(2):
        left = (wet_s[row, 0] > 0).astype(jnp.float32)
        right = (wet_s[row, 1] > 0).astype(jnp.float32)
        wet_ref[8 * row : 8 * row + 8, :] = jnp.where(lane < lanes // 2, left, right)
    for f in range(NF):
        sign = -1.0 if f in (QY, CY) else 1.0
        t = top_rows(top[f] if f < WET else wet_ref[0:8, :], COUNT[f], gy == 0, sign)
        b = bottom_rows(bot[f] if f < WET else wet_ref[8:16, :], COUNT[f], gy == ny - 1, sign)
        a_ref[sent(f), :] = jnp.where(even, b, t)
        b_ref[sent(f), :] = jnp.where(even, t, b)


def tile_wet(wet_ref, j, n):
    return wet_ref[rows(j // (n // 2)), :] > 0.5


def forward_kernel(wet_ref, w_ref, z_ref, lr_ref, c_ref, scr, across, adj, pg, rs_ref, tl_ref, tr_ref, sh, across0, zs):
    height, lanes = z_ref.shape
    n = height // BLK

    def field(f):
        if f <= QY:
            return w_ref.at[f]
        return z_ref if f == Z else lr_ref if f == LR else c_ref.at[f - CH]

    def get(f, j):
        return field(f)[rows(j), :]

    def wet(j):
        return tile_wet(wet_ref, j, n)

    first_pass(get, wet, n, scr, sh.at[0], across0, zs, second_parts(scr, sh.at[1], across))
    second_pass(get, wet, n, sh.at[1], across, adj, pg)
    lane = lax.broadcasted_iota(jnp.int32, (height, 128), 1)
    for f in range(WET):
        ref = field(f)
        rs_ref[f, 0:8, :] = ref[0:8, :]
        rs_ref[f, 8:16, :] = ref[height - 8 : height, :]
        turned = jnp.where(lane < 64, ref[:, 0:128], ref[:, lanes - 128 : lanes]).T
        tl_ref[f] = turned[0:8, :]
        tr_ref[f] = turned[120:128, :]
    top, bottom = wet_ref[0:8, :], wet_ref[8:16, :]
    rs_ref[WET, 0:8, :] = top
    rs_ref[WET, 8:16, :] = bottom
    half = lanes // 2
    tl_ref[WET] = jnp.concatenate([top[:, :half], bottom[:, :half]], 1)
    tr_ref[WET] = jnp.concatenate([top[:, half:], bottom[:, half:]], 1)


def strip_gradient(s_ref, scr, sh, ac, adj, pg, g_ref):
    n = s_ref.shape[1] // BLK

    def get(f, j):
        return s_ref[f, rows(j), :]

    def wet(j):
        return get(WET, j) > 0.5

    def put_grad(j, value):
        g_ref[rows(j), :] = value

    first_pass(get, wet, n, scr, sh.at[0], ac.at[0], adj, second_parts(scr, sh.at[1], ac.at[1]))
    second_pass(get, wet, n, sh.at[1], ac.at[1], adj, pg)
    third_pass((1, 2), scr, ac.at[1], adj, pg, put_grad)


def arctan_ratio(y, x):
    a = jnp.abs(y)
    big, small = jnp.maximum(a, x), jnp.minimum(a, x)
    far = small > 0.41421356 * big
    t = jnp.where(far, small - big, small) / jnp.where(far, small + big, big)
    z = t * t
    p = ((8.05374449538e-2 * z - 1.38776856032e-1) * z + 1.99777106478e-1) * z - 3.33329491539e-1
    r = p * z * t + t + jnp.where(far, math.pi / 4, 0.0)
    r = jnp.where(a > x, math.pi / 2 - r, r)
    return jnp.where(y < 0, -r, r)


def updated(g, rough, moment, second):
    nm = BETA_ONE * moment + (1.0 - BETA_ONE) * g
    nv = BETA_TWO * second + (1.0 - BETA_TWO) * g * g
    root = jnp.sqrt(nv * (1.0 / (1.0 - BETA_TWO**UPDATES)))
    turn = arctan_ratio(nm * (1.0 / (1.0 - BETA_ONE**UPDATES)), root)
    return rough - (LEARN_RATE * ATAN_SCALE) * turn, nm, nv


def backward_kernel(
    after_ref, ya_ref, yb_ref, yw_ref, rs_ref, scr, across, adj, pg, lr_ref, m_ref, v_ref,
    nr_ref, nm_ref, nv_ref, ml_ref, mr_ref, g_ref, row_s, row_scr, row_sh, row_ac, row_adj, row_pg, row_g,
):
    gy, ny = place("gy")
    even_y, at_wall_y = gy % 2 == 0, (gy == 0) | (gy == ny - 1)
    height, lanes = lr_ref.shape

    def put_grad(j, value):
        g_ref[rows(j), :] = value

    third_pass(height // BLK, scr, across, adj, pg, put_grad)
    for f in range(NF):
        r, c = sent(f), COUNT[f]
        ya, yb = ya_ref[r, :], jnp.where(at_wall_y, yw_ref[r, :], yb_ref[r, :])
        row_s[f, 0:8, :] = jnp.ones((8, lanes), jnp.float32)
        row_s[f, 24:32, :] = jnp.ones((8, lanes), jnp.float32)
        row_s[f, 8 - c : 8, :] = jnp.where(even_y, yb, ya)
        row_s[f, 24 : 24 + c, :] = jnp.where(even_y, ya, yb)
        row_s[f, 8:24, :] = rs_ref[f]
    strip_gradient(row_s, row_scr, row_sh, row_ac, row_adj, row_pg, row_g)
    row = lax.broadcasted_iota(jnp.int32, (8, lanes), 0)
    g_ref[0:8, :] = jnp.where(row < 3, row_g[8:16, :], g_ref[0:8, :])
    g_ref[height - 8 : height, :] = jnp.where(row >= 5, row_g[16:24, :], g_ref[height - 8 : height, :])

    def update(j):
        r = rows(j)
        nr_ref[r, :], nm_ref[r, :], nv_ref[r, :] = updated(
            g_ref[r, :], lr_ref[r, :], m_ref[r, :], v_ref[r, :]
        )

    looped(height // BLK, update)
    lane = lax.broadcasted_iota(jnp.int32, (height, 128), 1)
    for f, ref in enumerate((m_ref, v_ref)):
        turned = jnp.where(lane < 64, ref[:, 0:128], ref[:, lanes - 128 : lanes]).T
        ml_ref[f] = turned[0:8, :]
        mr_ref[f] = turned[120:128, :]


def pack_cols_kernel(yb_ref, ya_ref, yw_ref, tl_ref, tr_ref, b_ref, a_ref, pl_ref, pr_ref, k_scr):
    gx, nx = place("gx")
    gy, ny = place("gy")
    even_y = gy % 2 == 0
    lanes = ya_ref.shape[1]
    y_b = jnp.where((gy == 0) | (gy == ny - 1), yw_ref[...], yb_ref[...])
    below = jnp.where(even_y, ya_ref[...], y_b)
    above = jnp.where(even_y, y_b, ya_ref[...])
    lane = lax.broadcasted_iota(jnp.int32, (above.shape[0], 128), 1)
    above = jnp.where(lane < 64, above[:, 0:128], above[:, lanes - 128 : lanes])
    below = jnp.where(lane < 64, below[:, 0:128], below[:, lanes - 128 : lanes])
    k_scr[...] = jnp.zeros_like(k_scr)
    for f in range(NF):
        c = 3 if f == WET else COUNT[f]
        k_scr[6 * f + 3 - c : 6 * f + 3, :] = jnp.broadcast_to(above[sent(f), :], (c, 128))
        k_scr[6 * f + 3 : 6 * f + 3 + c, :] = jnp.broadcast_to(below[sent(f), :], (c, 128))
    turned = k_scr[...].T
    left_corner, right_corner = turned[0:8, :], turned[120:128, :]
    pl_ref[...] = left_corner
    pr_ref[...] = right_corner
    even = gx % 2 == 0
    a_ref[...] = jnp.zeros_like(a_ref)
    b_ref[...] = jnp.zeros_like(b_ref)
    first, last = gx == 0, gx == nx - 1
    for f in range(NF):
        sign = -1.0 if f in (QX, CX) else 1.0
        t = top_rows(tl_ref[f], COUNT[f], first, sign)
        b = bottom_rows(tr_ref[f], COUNT[f], last, sign)
        a_ref[sent(f), :] = jnp.where(even, b, t)
        b_ref[sent(f), :] = jnp.where(even, t, b)
    lane = lax.broadcasted_iota(jnp.int32, (3, 128), 1)
    flip = ((lane >= 6 * QX) & (lane < 6 * QX + 6)) | ((lane >= 6 * CX) & (lane < 6 * CX + 6))
    sign = jnp.where(flip, -1.0, 1.0)
    t = top_rows(left_corner, 3, first, sign)
    b = bottom_rows(right_corner, 3, last, sign)
    a_ref[SENT : SENT + 3, 0:128] = jnp.where(even, b, t)
    b_ref[SENT : SENT + 3, 0:128] = jnp.where(even, t, b)


def rim_kernel(
    xa_ref, xb_ref, xw_ref, tl_ref, tr_ref, pl_ref, pr_ref, ml_ref, mr_ref, ir_ref, im_ref, iv_ref,
    nr_ref, nm_ref, nv_ref, col_s, col_scr, col_sh, col_ac, col_adj, col_pg, col_g, turn_scr,
):
    gx, nx = place("gx")
    even_x, at_wall_x = gx % 2 == 0, (gx == 0) | (gx == nx - 1)
    height, lanes = ir_ref.shape
    x_b = jnp.where(at_wall_x, xw_ref[...], xb_ref[...])
    left_in = jnp.where(even_x, x_b, xa_ref[...])
    right_in = jnp.where(even_x, xa_ref[...], x_b)
    for f, t in enumerate(TURNED):
        shift = (125 - 6 * f) % 128
        r, c = sent(f), COUNT[f]
        col_s[t, 0:8, :] = jnp.ones((8, height + 128), jnp.float32)
        col_s[t, 24:32, :] = jnp.ones((8, height + 128), jnp.float32)
        col_s[t, 8 - c : 8, 0:height] = left_in[r, :]
        col_s[t, 24 : 24 + c, 0:height] = right_in[r, :]
        col_s[t, 8:16, 0:height] = tl_ref[f]
        col_s[t, 16:24, 0:height] = tr_ref[f]
        col_s[t, 5:8, height:] = pltpu.roll(left_in[16:24, 0:128], shift, 1)[2:5, :]
        col_s[t, 24:27, height:] = pltpu.roll(right_in[16:24, 0:128], shift, 1)[2:5, :]
        col_s[t, 8:16, height:] = pltpu.roll(pl_ref[...], shift, 1)
        col_s[t, 16:24, height:] = pltpu.roll(pr_ref[...], shift, 1)
    strip_gradient(col_s, col_scr, col_sh, col_ac, col_adj, col_pg, col_g)
    turn_scr[:, 8:120, :] = jnp.zeros((3, 112, height), jnp.float32)
    for r, g, t_ref, s_ref in ((slice(0, 8), 8, tl_ref, ml_ref), (slice(120, 128), 16, tr_ref, mr_ref)):
        new = updated(col_g[g : g + 8, 0:height], t_ref[LR], s_ref[0], s_ref[1])
        for f in range(3):
            turn_scr[f, r, :] = new[f]
    lane = lax.broadcasted_iota(jnp.int32, (height, 128), 1)
    for f, (src, dst) in enumerate(((ir_ref, nr_ref), (im_ref, nm_ref), (iv_ref, nv_ref))):
        side = turn_scr[f].T
        dst[:, 0:128] = jnp.where(lane < 3, side, src[:, 0:128])
        dst[:, lanes - 128 : lanes] = jnp.where(lane >= 125, side, src[:, lanes - 128 : lanes])


def swap_pairs(nx, ny, axis, odd):
    pairs = []
    for x in range(nx):
        for y in range(ny):
            u, v = x, y
            if axis == "gx":
                u = x ^ 1 if not odd else ((x + 1) ^ 1) - 1
                if not 0 <= u < nx:
                    u, v = x, y ^ 1
            else:
                v = y ^ 1 if not odd else ((y + 1) ^ 1) - 1
                if not 0 <= v < ny:
                    u, v = x ^ 1, y
            pairs.append((x * ny + y, u * ny + v))
    return pairs


def swapped(value, axis, odd):
    pairs = swap_pairs(lax.axis_size("gx"), lax.axis_size("gy"), axis, odd)
    return lax.ppermute(value, ("gx", "gy"), pairs)


def call(kernel, out_shapes, scratch=(), in_specs=None, flops=0, vmem_mb=VMEM_MB):
    params = pltpu.CompilerParams(vmem_limit_bytes=vmem_mb << 20)
    shapes = [jax.ShapeDtypeStruct(s, jnp.float32) for s in out_shapes]
    kwargs = {} if in_specs is None else {"in_specs": in_specs}
    return pl.pallas_call(
        kernel,
        out_shape=shapes,
        scratch_shapes=list(scratch),
        compiler_params=params,
        cost_estimate=pl.CostEstimate(flops=flops, bytes_accessed=flops // 8, transcendentals=0),
        **kwargs,
    )


def on_device(water, ground, rough, moment, second, wet_tiles, cot):
    height, lanes = ground.shape
    hbm = pl.BlockSpec(memory_space=pltpu.HBM)
    y_b, y_a, wet = call(
        pack_rows_kernel,
        [(24, lanes), (24, lanes), (16, lanes)],
        scratch=[
            pltpu.SMEM((2, 2), jnp.int32),
            pltpu.VMEM((8, 8, lanes), jnp.float32),
            pltpu.VMEM((8, 8, lanes), jnp.float32),
            pltpu.SemaphoreType.DMA((9,)),
        ],
        in_specs=[hbm] * 5,
        vmem_mb=12,
    )(*(pltpu.with_memory_space_constraint(x, pltpu.HBM) for x in (wet_tiles, water, ground, rough, cot)))
    y_wall, y_b, y_a = y_b, swapped(y_b, "gy", True), swapped(y_a, "gy", False)
    kept = [
        (N_AHEAD, height, lanes),
        (N_ACROSS, height, lanes),
        (3, lanes // 128, height + 16, 128),
        (height, lanes),
    ]
    scr, across, adj, pg, row_own, col_left, col_right = call(
        forward_kernel,
        [*kept, (NF, 16, lanes), (NF, 8, height), (NF, 8, height)],
        scratch=[
            pltpu.VMEM((2, N_SHIFTED, lanes // 128, height + 16, 128), jnp.float32),
            pltpu.VMEM((N_ACROSS, height, lanes), jnp.float32),
            pltpu.VMEM((1, lanes // 128, height + 16, 128), jnp.float32),
        ],
        flops=20_000_000,
    )(wet, water, ground, rough, cot)
    x_b, x_a, corner_left, corner_right = call(
        pack_cols_kernel,
        [(24, height), (24, height), (8, 128), (8, 128)],
        scratch=[pltpu.VMEM((128, 128), jnp.float32)],
    )(y_b, y_a, y_wall, col_left, col_right)
    own_rough, own_moment, own_second, mom_left, mom_right = call(
        backward_kernel,
        [(height, lanes)] * 3 + [(2, 8, height)] * 2,
        scratch=[
            pltpu.VMEM((height, lanes), jnp.float32),
            pltpu.VMEM((NF, 32, lanes), jnp.float32),
            pltpu.VMEM((N_AHEAD, 32, lanes), jnp.float32),
            pltpu.VMEM((2, N_SHIFTED, lanes // 128, 48, 128), jnp.float32),
            pltpu.VMEM((2, N_ACROSS, 32, lanes), jnp.float32),
            pltpu.VMEM((3, lanes // 128, 48, 128), jnp.float32),
            pltpu.VMEM((32, lanes), jnp.float32),
            pltpu.VMEM((32, lanes), jnp.float32),
        ],
        flops=20_000_000,
    )(corner_left, y_a, y_b, y_wall, row_own, scr, across, adj, pg, rough, moment, second)
    x_wall, x_b, x_a = x_b, swapped(x_b, "gx", True), swapped(x_a, "gx", False)
    return tuple(
        call(
            rim_kernel,
            [(height, lanes)] * 3,
            scratch=[
                pltpu.VMEM((NF, 32, height + 128), jnp.float32),
                pltpu.VMEM((N_AHEAD, 32, height + 128), jnp.float32),
                pltpu.VMEM((2, N_SHIFTED, height // 128 + 1, 48, 128), jnp.float32),
                pltpu.VMEM((2, N_ACROSS, 32, height + 128), jnp.float32),
                pltpu.VMEM((3, height // 128 + 1, 48, 128), jnp.float32),
                pltpu.VMEM((32, height + 128), jnp.float32),
                pltpu.VMEM((32, height + 128), jnp.float32),
                pltpu.VMEM((3, 128, height), jnp.float32),
            ],
        )(
            x_a, x_b, x_wall, col_left, col_right, corner_left, corner_right,
            mom_left, mom_right, own_rough, own_moment, own_second,
        )
    )


def solution(mesh):
    flat = P("gy", "gx")
    deep = P(None, "gy", "gx")

    return jax.shard_map(
        on_device,
        mesh=mesh,
        in_specs=(deep, flat, flat, flat, flat, flat, deep),
        out_specs=(flat, flat, flat),
        check_vma=False,
    )
```
